128 devices in a mesh: off: 2 (over core), win: 64 (over y, z, x).
Axes of the slice: x: 4, y: 4, z: 4, core: 2. Of those that a mesh axis runs over, the one named last changes fastest.
Arguments:
- kernels: float32 [2, 64, 64, 64, 128], P('off', 'win'), may hold values from -6 to 6
- blocks: int32 [2, 64, 64, 128], P('off', 'win'), may hold values from 0 to 2047
- counts: int32 [2, 64, 64], P('off', 'win'), may hold values from 1 to 128, as said below
- ray_of: int32 [2, 64, 64, 128], P('off', 'win'), may hold values from 0 to 511
- slopes: float32 [2, 64, 512], P('off', 'win'), may hold values from -6 to 6
Outputs:
- update: float32 [64, 131072], P(None, 'win')
- data_vector: float32 [2, 64, 512], P('off', 'win')
The draws below stay inside these ranges and needn't reach their ends.
Inputs may be any that keep to these rules, and one draw needn't show every extreme that they name: `counts`: some event windows, drawn from the seed (each with chance one in four), carry more segments each than the rest; one owner, drawn from the seed, receives 128 live slots from every window of every offset class.
All inputs are finite; a program needn't handle non-finite values.
Results may differ from the reference program's by a relative error of at most 0.0003.
Values sent between devices are 32-bit elements; how exact they have to be, the bound alone decides.
No kernel may reach another device: no remote copies, remote signals or barrier semaphores. Data moves between devices by JAX's collectives and lax.ppermute only.
A program may use at most 64 MiB of HBM per device.

```python
import jax
import jax.numpy as jnp
from jax import lax

CELLS = 64
CAP = 128
BLK_DEV = 2048
RAYS = 512
ITERS = 3
NBLK = 131072
N_OFF = 2
N_WIN = 64


def draw_counts(key, part):
    keys = jax.random.split(jax.random.fold_in(key, 7), 4)
    shape = (N_OFF, N_WIN, N_WIN)
    heavy = jax.random.randint(keys[0], (N_OFF, N_WIN, 1), 0, 4) == 0
    upper = jax.random.randint(keys[1], shape, CAP // 2, CAP + 1)
    lower = jax.random.randint(keys[2], shape, 1, max(1, CAP // 4) + 1)
    loads = jnp.where(heavy, upper, lower)
    full_owner = jax.random.randint(keys[3], (), 0, N_WIN)
    owners = jnp.arange(N_WIN, dtype=jnp.int32)[None, None, :]
    return jnp.where(owners == full_owner, CAP, loads).astype(jnp.int32)


def with_ends(result, rng, least, largest):
    index_at = [jax.random.randint(jax.random.fold_in(rng, axis), (), 0, length) for axis, length in enumerate(result.shape)]
    widest = result.shape.index(max(result.shape))
    beside = index_at[:widest] + [(index_at[widest] + 1) % result.shape[widest]] + index_at[widest + 1:]
    return result.at[tuple(index_at)].set(least).at[tuple(beside)].set(largest)


def block_levels(rng, extent, shards, smallest, largest):
    gain, own = 1.0, jax.random.fold_in(rng, 6)
    for dim, parts in shards:
        draws = jnp.exp(jax.random.uniform(jax.random.fold_in(own, dim), (parts,), jnp.float32, smallest / len(shards), largest / len(shards)))
        gain = gain * jnp.repeat(draws, extent[dim] // parts).reshape([-1 if axis == dim else 1 for axis in range(len(extent))])
    return gain


def bell_draw(key, extent, width, most, cuts=(), held_as=jnp.bfloat16):
    result = jax.random.normal(key, extent, jnp.float32) * width
    if len(cuts) > 0:
        result = block_levels(key, extent, cuts, -0.22, 0.18) * result
    return jnp.clip(result, min=-most, max=most).astype(held_as)


def setup_inputs(seed: int = 0) -> dict:
    key_of = jax.random.split(jax.random.key(seed), 6)
    kernels = bell_draw(key_of[0], (N_OFF, N_WIN, N_WIN, CELLS, CAP), 1.0, 6.0, ((0, 2), (1, 64)), jnp.float32)
    blocks = with_ends(jax.random.randint(key_of[1], (N_OFF, N_WIN, N_WIN, CAP), 0, BLK_DEV), jax.random.fold_in(key_of[1], 1), 0, BLK_DEV - 1).astype(jnp.int32)
    counts = draw_counts(jax.random.fold_in(key_of[5], 71), 0)
    ray_of = with_ends(jax.random.randint(key_of[3], (N_OFF, N_WIN, N_WIN, CAP), 0, RAYS), jax.random.fold_in(key_of[3], 1), 0, RAYS - 1).astype(jnp.int32)
    slopes = bell_draw(key_of[4], (N_OFF, N_WIN, RAYS), 1.0, 6.0, ((0, 2), (1, 64)), jnp.float32)
    return {"kernels": kernels, "blocks": blocks, "counts": counts, "ray_of": ray_of, "slopes": slopes}


def masked_rows(kernel_src, count_src):
    slots = lax.broadcasted_iota(jnp.int32, kernel_src.shape, 2)
    return jnp.where(slots < count_src[:, None, None], kernel_src, jnp.zeros_like(kernel_src))

def global_ids(block_src):
    owners = lax.broadcasted_iota(jnp.int32, block_src.shape, 0)
    return (owners * BLK_DEV + block_src).astype(jnp.int32)

def reference(kernels, blocks, counts, ray_of, slopes):
    sources = N_OFF * N_WIN
    kern_all = kernels.reshape(sources, N_WIN, CELLS, CAP)
    block_all = blocks.reshape(sources, N_WIN, CAP)
    count_all = counts.reshape(sources, N_WIN)
    ray_all = ray_of.reshape(sources, N_WIN, CAP)

    def forward(model):

        def one_source(packed):
            kernel_src, block_src, count_src, ray_src = packed
            rows = masked_rows(kernel_src, count_src)
            fetched = jnp.moveaxis(model[:, global_ids(block_src)], 0, 1)
            values = lax.optimization_barrier(jnp.sum(rows * fetched, axis=1))
            return jax.ops.segment_sum(values.reshape(-1), ray_src.reshape(-1), num_segments=RAYS)
        data = lax.map(one_source, (kern_all, block_all, count_all, ray_all))
        return data.reshape(N_OFF, N_WIN, RAYS)

    def adjoint(data):
        data_src = data.reshape(sources, RAYS)

        def one_source(grad, packed):
            kernel_src, block_src, count_src, ray_src, datum = packed
            rows = masked_rows(kernel_src, count_src)
            weights = datum[ray_src]
            contrib = jnp.moveaxis(rows * weights[:, None, :], 1, 0).reshape(CELLS, -1)
            grad = grad.at[:, global_ids(block_src).reshape(-1)].add(contrib)
            return (grad, None)
        start = jnp.zeros((CELLS, NBLK), jnp.float32)
        grad, unused = lax.scan(one_source, start, (kern_all, block_all, count_all, ray_all, data_src))
        return grad
    beta = jnp.sqrt(jnp.sum(slopes * slopes))
    data_vector = slopes / beta
    model_vec = adjoint(data_vector)
    alpha = jnp.sqrt(jnp.sum(model_vec * model_vec))
    model_vec = model_vec / alpha
    search = model_vec
    phibar = beta
    rhobar = alpha
    update = jnp.zeros((CELLS, NBLK), jnp.float32)
    for step in range(ITERS):
        data_vector = forward(model_vec) - alpha * data_vector
        beta = jnp.sqrt(jnp.sum(data_vector * data_vector))
        data_vector = data_vector / beta
        model_vec = adjoint(data_vector) - beta * model_vec
        alpha = jnp.sqrt(jnp.sum(model_vec * model_vec))
        model_vec = model_vec / alpha
        rho = jnp.sqrt(rhobar * rhobar + beta * beta)
        cosine = rhobar / rho
        sine = beta / rho
        theta = sine * alpha
        rhobar = -cosine * alpha
        phi = cosine * phibar
        phibar = sine * phibar
        update = update + phi / rho * search
        search = model_vec - theta / rho * search
    return (update, data_vector)
```

```python
import functools

import jax
import jax.numpy as jnp
from jax import lax
from jax.experimental import pallas as pl
from jax.experimental.pallas import tpu as pltpu
from jax.sharding import PartitionSpec as P

CELLS = 64
CAP = 128
BLK_DEV = 2048
RAYS = 512
ITERS = 3
N_OFF = 2
N_WIN = 64
SRC = N_OFF * N_WIN
CC = CELLS // N_OFF
RT = RAYS // 128
HI = 8
LO = BLK_DEV // HI
CH = 8
F32 = jnp.float32
BF16 = jnp.bfloat16


def rows(ref, start, count, stride):
    return ref[pl.ds(start, count, stride=stride), :]


def gather_rays(data, ray, out_ref, stride, first):
    lo = jnp.bitwise_and(ray, 127)
    hi = jnp.right_shift(ray, 7)
    parts = []
    for g in range(N_WIN // 8):
        lo_g, hi_g = lo[g * 8 : g * 8 + 8], hi[g * 8 : g * 8 + 8]
        acc = jnp.zeros((8, 128), F32)
        for t in range(RT):
            table = jnp.broadcast_to(data[t : t + 1], (8, 128))
            got = jnp.take_along_axis(table, lo_g, axis=1, mode="promise_in_bounds")
            acc = jnp.where(hi_g == t, got, acc)
        parts.append(acc)
    weights = jnp.concatenate(parts, axis=0)
    out_ref[pl.ds(first, N_WIN, stride=2 * stride), :] = weights
    out_ref[pl.ds(first + stride, N_WIN, stride=2 * stride), :] = weights


def start_kernel(blocks_ref, counts_ref, ray_ref, slopes_ref, out_ref):
    slot = lax.broadcasted_iota(jnp.int32, (N_WIN, CAP), 1)
    ids = jnp.where(slot < counts_ref[...], blocks_ref[...], -1).astype(F32)
    out_ref[pl.ds(0, N_WIN, stride=6), :] = ids
    out_ref[pl.ds(3, N_WIN, stride=6), :] = ids
    data = slopes_ref[...]
    gather_rays(data, ray_ref[...], out_ref, 3, 1)
    out_ref[pl.ds(2, SRC, stride=3), :] = jnp.full((SRC, 128), jnp.sum(data * data), F32)


def start_call(blocks, counts, ray, slopes):
    return pl.pallas_call(
        start_kernel,
        out_shape=jax.ShapeDtypeStruct((3 * SRC, 128), F32),
        name="start",
    )(blocks, counts, ray, slopes)


def owner_kernel(first, k_ref, blk_ref, wts_ref, pprev_ref, aprev_ref, *refs):
    if first:
        p_ref, vals_ref, beta_ref, ids_ref, oh_ref, y_ref, acc_ref = refs
        ids_ref[...] = rows(blk_ref, 0, SRC, 3).astype(jnp.int32)
    else:
        p_ref, vals_ref, beta_ref, oh_ref, y_ref, acc_ref = refs
        ids_ref = blk_ref
    stride = wts_ref.shape[0] // SRC
    norm = jnp.sum(rows(wts_ref, stride - 1, SRC, stride), axis=0, keepdims=True)
    beta = jnp.sqrt(norm)
    beta_ref[...] = beta
    acc_ref[...] = jnp.zeros_like(acc_ref)
    lo_iota = lax.broadcasted_iota(jnp.int32, (LO, 128), 0)

    def chunk(i, carry):
        for c in range(CH):
            s = i * CH + c
            at = slice(c * 128, (c + 1) * 128)
            blk = ids_ref[pl.ds(s, 1), :]
            lo = jnp.where(blk < 0, -1, jnp.bitwise_and(blk, LO - 1))
            hi = jnp.right_shift(blk, 8)
            hit = lo_iota == jnp.broadcast_to(lo, (LO, 128))
            oh_ref[:, at] = jnp.where(hit, 1.0, 0.0).astype(BF16)
            weight = wts_ref[pl.ds(stride * s + stride - 2, 1), :]
            x = k_ref[s] * jnp.broadcast_to(weight, (CC, 128))
            x1 = x.astype(BF16).astype(F32)
            x2 = x - x1
            hib = jnp.broadcast_to(hi, (CC, 128))
            for h in range(HI):
                m = hib == h
                y_ref[2 * h * CC : (2 * h + 1) * CC, at] = jnp.where(m, x1, 0.0).astype(BF16)
                y_ref[(2 * h + 1) * CC : (2 * h + 2) * CC, at] = jnp.where(m, x2, 0.0).astype(BF16)
        acc_ref[...] += lax.dot_general(
            y_ref[...], oh_ref[...], (((1,), (1,)), ((), ())), preferred_element_type=F32
        )
        return carry

    lax.fori_loop(0, SRC // CH, chunk, 0)
    squares = jnp.zeros((8, 128), F32)
    beta_b = jnp.broadcast_to(beta, (CC, 128))
    if not first:
        back = jnp.broadcast_to(beta / aprev_ref[...], (CC, 128))
    for h in range(HI):
        for t in range(LO // 128):
            at = slice(t * 128, (t + 1) * 128)
            g = acc_ref[2 * h * CC : (2 * h + 1) * CC, at] + acc_ref[(2 * h + 1) * CC : (2 * h + 2) * CC, at]
            g = g / beta_b
            cols = slice(h * LO + t * 128, h * LO + (t + 1) * 128)
            if not first:
                g = g - pprev_ref[:, cols] * back
            p_ref[:, cols] = g
            g2 = g * g
            squares = squares + g2[0:8] + g2[8:16] + g2[16:24] + g2[24:32]
    vals_ref[pl.ds(1, SRC, stride=2), :] = jnp.full((SRC, 128), jnp.sum(squares), F32)

    def fetch(s, carry):
        blk = jnp.broadcast_to(ids_ref[pl.ds(s, 1), :], (8, 128))
        lo = jnp.bitwise_and(blk, 127)
        hi = jnp.right_shift(blk, 7)
        accs = [jnp.zeros((8, 128), F32) for _ in range(CC // 8)]
        for h in range(BLK_DEV // 128):
            m = hi == h
            for j in range(CC // 8):
                table = p_ref[j * 8 : j * 8 + 8, h * 128 : h * 128 + 128]
                got = jnp.take_along_axis(table, lo, axis=1, mode="promise_in_bounds")
                accs[j] = jnp.where(m, got, accs[j])
        total = k_ref[s, 0:8, :] * accs[0]
        for j in range(1, CC // 8):
            total = total + k_ref[s, j * 8 : j * 8 + 8, :] * accs[j]
        vals_ref[pl.ds(2 * s, 1), :] = jnp.sum(total, axis=0, keepdims=True)
        return carry

    lax.fori_loop(0, SRC, fetch, 0, unroll=2)


def owner_call(first, k, ids, weights, prev, alpha):
    outs = [
        jax.ShapeDtypeStruct((CC, BLK_DEV), F32),
        jax.ShapeDtypeStruct((2 * SRC, 128), F32),
        jax.ShapeDtypeStruct((1, 128), F32),
    ]
    if first:
        outs.append(jax.ShapeDtypeStruct((SRC, 128), jnp.int32))
    return pl.pallas_call(
        functools.partial(owner_kernel, first),
        out_shape=tuple(outs),
        scratch_shapes=[
            pltpu.VMEM((LO, CH * 128), BF16),
            pltpu.VMEM((2 * HI * CC, CH * 128), BF16),
            pltpu.VMEM((2 * HI * CC, LO), F32),
        ],
        compiler_params=pltpu.CompilerParams(vmem_limit_bytes=48 << 20),
        name="owner",
    )(k, ids, weights, prev, alpha)


def window_kernel(vals_ref, ray_ref, q_ref, beta_ref, wts_ref, qout_ref, alpha_ref, norm_ref, a_ref, b_ref):
    alpha = jnp.sqrt(jnp.sum(rows(vals_ref, 1, SRC, 2), axis=0, keepdims=True))
    alpha_ref[...] = alpha
    vals = rows(vals_ref, 0, N_WIN, 4) + rows(vals_ref, 2, N_WIN, 4)
    v1 = vals.astype(BF16).astype(F32)
    v2 = (vals - v1).astype(BF16).astype(F32)
    v3 = vals - v1 - v2
    ray = ray_ref[...]
    lo = jnp.bitwise_and(ray, 127)
    hi = jnp.right_shift(ray, 7)
    sub = lax.broadcasted_iota(jnp.int32, (8, 128), 0)
    tier = jnp.bitwise_and(sub, RT - 1)
    lo_iota = lax.broadcasted_iota(jnp.int32, (128, 128), 0)
    wide = lambda r, p, n: jnp.broadcast_to(r[p : p + 1], (n, 128))
    for p in range(N_WIN):
        at = slice(p * 128, (p + 1) * 128)
        hit = tier == wide(hi, p, 8)
        upper = jnp.where(sub < RT, wide(v1, p, 8), wide(v2, p, 8))
        lower = jnp.where(sub < RT, wide(v3, p, 8), 0.0)
        both = jnp.concatenate([jnp.where(hit, upper, 0.0), jnp.where(hit, lower, 0.0)], axis=0)
        a_ref[:, at] = both.astype(BF16)
        b_ref[:, at] = jnp.where(lo_iota == wide(lo, p, 128), 1.0, 0.0).astype(BF16)
    out = lax.dot_general(a_ref[...], b_ref[...], (((1,), (1,)), ((), ())), preferred_element_type=F32)
    summed = out[0:RT] + out[RT : 2 * RT] + out[2 * RT : 3 * RT]
    alpha_b = jnp.broadcast_to(alpha, (RT, 128))
    beta_b = jnp.broadcast_to(beta_ref[...], (RT, 128))
    q = summed / alpha_b - alpha_b * (q_ref[...] / beta_b)
    qout_ref[...] = q
    part = jnp.sum(q * q)
    gather_rays(q, ray, wts_ref, 2, 0)
    wts_ref[pl.ds(1, SRC, stride=2), :] = jnp.full((SRC, 128), part, F32)
    norm_ref[...] = jnp.full((SRC, 128), part, F32)


def window_call(vals, ray, q, beta):
    return pl.pallas_call(
        window_kernel,
        out_shape=(
            jax.ShapeDtypeStruct((2 * SRC, 128), F32),
            jax.ShapeDtypeStruct((RT, 128), F32),
            jax.ShapeDtypeStruct((1, 128), F32),
            jax.ShapeDtypeStruct((SRC, 128), F32),
        ),
        scratch_shapes=[
            pltpu.VMEM((16, N_WIN * 128), BF16),
            pltpu.VMEM((128, N_WIN * 128), BF16),
        ],
        compiler_params=pltpu.CompilerParams(vmem_limit_bytes=16 << 20),
        name="window",
    )(vals, ray, q, beta)


def end_kernel(norm_ref, q_ref, *refs):
    mine, theirs = refs[0:ITERS], refs[ITERS : 2 * ITERS]
    alphas = [r[...] for r in refs[2 * ITERS : 3 * ITERS]]
    betas = [r[...] for r in refs[3 * ITERS : 4 * ITERS]]
    update_ref, data_ref = refs[4 * ITERS :]
    betas.append(jnp.sqrt(jnp.sum(norm_ref[...], axis=0, keepdims=True)))
    data_ref[...] = q_ref[...] / jnp.broadcast_to(betas[ITERS], (RT, 128))
    one = jnp.ones_like(alphas[0])
    phibar, rhobar = betas[0], alphas[0]
    search = [one]
    update = [jnp.zeros_like(one) for _ in range(ITERS)]
    for step in range(ITERS):
        beta = betas[step + 1]
        rho = jnp.sqrt(rhobar * rhobar + beta * beta)
        cosine = rhobar / rho
        sine = beta / rho
        phi = cosine * phibar
        phibar = sine * phibar
        for i, s in enumerate(search):
            update[i] = update[i] + phi / rho * s
        if step + 1 < ITERS:
            theta = sine * alphas[step + 1]
            rhobar = -cosine * alphas[step + 1]
            search = [-(theta / rho * s) for s in search] + [one]
    scale = [jnp.broadcast_to(u / a, (CC, 128)) for u, a in zip(update, alphas)]
    core = lax.axis_index("off")
    for refs_in, half in ((mine, core), (theirs, 1 - core)):
        at = pl.ds(pl.multiple_of(half * CC, CC), CC)
        for t in range(BLK_DEV // 128):
            cols = slice(t * 128, (t + 1) * 128)
            total = refs_in[0][:, cols] * scale[0]
            for i in range(1, ITERS):
                total = total + refs_in[i][:, cols] * scale[i]
            update_ref[at, cols] = total


def end_call(norm, q, mine, theirs, alphas, betas):
    return pl.pallas_call(
        end_kernel,
        out_shape=(
            jax.ShapeDtypeStruct((CELLS, BLK_DEV), F32),
            jax.ShapeDtypeStruct((RT, 128), F32),
        ),
        compiler_params=pltpu.CompilerParams(vmem_limit_bytes=16 << 20),
        name="end",
    )(norm, q, *mine, *theirs, *alphas, *betas)


def exchange(x):
    rest = x.shape[0] // SRC
    y = lax.all_to_all(x.reshape(SRC, rest, 128), ("win", "off"), 0, 0, tiled=True)
    return y.reshape(x.shape)


def body(kernels, blocks, counts, ray_of, slopes):
    ray = ray_of.reshape(N_WIN, CAP)
    q = slopes.reshape(RT, 128)
    k = lax.all_to_all(kernels.reshape(SRC, CC, CAP), ("win", "off"), 0, 0, tiled=True)
    weights = exchange(start_call(blocks.reshape(N_WIN, CAP), counts.reshape(N_WIN, 1), ray, q))
    ids = weights
    prev, alpha = jnp.zeros((8, 128), F32), jnp.zeros((1, 128), F32)
    mine, theirs, alphas, betas = [], [], [], []
    for step in range(ITERS):
        out = owner_call(step == 0, k, ids, weights, prev, alpha)
        prev, vals, beta = out[:3]
        if step == 0:
            ids = out[3]
        mine.append(prev)
        theirs.append(lax.ppermute(prev, "off", [(0, 1), (1, 0)]))
        betas.append(beta)
        weights, q, alpha, norm = window_call(exchange(vals), ray, q, beta)
        alphas.append(alpha)
        weights = exchange(weights)
    owner_call(False, k, ids, weights, prev, alpha)
    update, data = end_call(exchange(norm), q, mine, theirs, alphas, betas)
    return update, data.reshape(1, 1, RAYS)


def solution(mesh):
    in_specs = (
        P("off", "win", None, None, None),
        P("off", "win", None, None),
        P("off", "win", None),
        P("off", "win", None, None),
        P("off", "win", None),
    )
    out_specs = (P(None, "win"), P("off", "win", None))
    return jax.shard_map(body, mesh=mesh, in_specs=in_specs, out_specs=out_specs, check_vma=False)
```

```python
import functools

import jax
import jax.numpy as jnp
from jax import lax
from jax.experimental import pallas as pl
from jax.experimental.pallas import tpu as pltpu
from jax.sharding import PartitionSpec as P

CELLS = 64
CAP = 128
BLK_DEV = 2048
RAYS = 512
ITERS = 3
N_OFF = 2
N_WIN = 64
SRC = N_OFF * N_WIN
CC = CELLS // N_OFF
RT = RAYS // 128
HI = 8
LO = BLK_DEV // HI
CA = 16
CF = 8
PACK = 4
F32 = jnp.float32
BF16 = jnp.bfloat16


def rows(ref, start, count, stride):
    return ref[pl.ds(start, count, stride=stride), :]


def gather_rays(data, ray, out_ref, stride, first):
    lo = jnp.bitwise_and(ray, 127)
    hi = jnp.right_shift(ray, 7)
    parts = []
    for g in range(N_WIN // 8):
        lo_g, hi_g = lo[g * 8 : g * 8 + 8], hi[g * 8 : g * 8 + 8]
        acc = jnp.zeros((8, 128), F32)
        for t in range(RT):
            table = jnp.broadcast_to(data[t : t + 1], (8, 128))
            got = jnp.take_along_axis(table, lo_g, axis=1, mode="promise_in_bounds")
            acc = jnp.where(hi_g == t, got, acc)
        parts.append(acc)
    weights = jnp.concatenate(parts, axis=0)
    out_ref[pl.ds(first, N_WIN, stride=2 * stride), :] = weights
    out_ref[pl.ds(first + stride, N_WIN, stride=2 * stride), :] = weights


def start_kernel(blocks_ref, counts_ref, ray_ref, slopes_ref, out_ref):
    slot = lax.broadcasted_iota(jnp.int32, (N_WIN, CAP), 1)
    row = lax.broadcasted_iota(jnp.int32, (N_WIN, N_WIN), 0)
    col = lax.broadcasted_iota(jnp.int32, (N_WIN, N_WIN), 1)
    counts = jnp.broadcast_to(counts_ref[...].astype(F32), (N_WIN, N_WIN))
    counts = jnp.sum(jnp.where(row == col, counts, 0.0), axis=1, keepdims=True)
    ids = jnp.where(slot.astype(F32) < counts, blocks_ref[...].astype(F32), -1.0)
    out_ref[pl.ds(0, N_WIN, stride=2 * PACK), :] = ids
    out_ref[pl.ds(PACK, N_WIN, stride=2 * PACK), :] = ids
    data = slopes_ref[...]
    gather_rays(data, ray_ref[...], out_ref, PACK, 1)
    part = jnp.full((SRC, 128), jnp.sum(data * data), F32)
    out_ref[pl.ds(2, SRC, stride=PACK), :] = part
    out_ref[pl.ds(3, SRC, stride=PACK), :] = part


def start_call(blocks, counts, ray, slopes):
    return pl.pallas_call(
        start_kernel,
        out_shape=jax.ShapeDtypeStruct((PACK * SRC, 128), F32),
        compiler_params=pltpu.CompilerParams(vmem_limit_bytes=4 << 20),
        name="start",
    )(blocks, counts, ray, slopes)


def owner_kernel(first, k_ref, ids_in_ref, wts_ref, pprev_ref, aprev_ref, *refs):
    if first:
        p_ref, vals_ref, beta_ref, ids_ref, *scratch = refs
        ids_ref[...] = rows(ids_in_ref, 0, SRC, PACK).astype(jnp.int32)
        stride, at_weight = PACK, 1
    else:
        p_ref, vals_ref, beta_ref, *scratch = refs
        ids_ref = ids_in_ref
        stride, at_weight = 2, 0
    oh_ref, y0_ref, y1_ref, acc_ref, v_ref, g0_ref, g1_ref = scratch
    beta = jnp.sqrt(jnp.sum(rows(wts_ref, at_weight + 1, SRC, stride), axis=0, keepdims=True))
    beta_ref[...] = beta
    acc_ref[...] = jnp.zeros_like(acc_ref)
    lo_iota = lax.broadcasted_iota(jnp.int32, (LO, 128), 0)

    def spread(y_ref, i):
        for c in range(CA):
            s = i * CA + c
            at = slice(c * 128, (c + 1) * 128)
            blk = ids_ref[pl.ds(s, 1), :]
            lo = jnp.where(blk < 0, -1, jnp.bitwise_and(blk, LO - 1))
            hi = jnp.right_shift(blk, 8)
            hit = lo_iota == jnp.broadcast_to(lo, (LO, 128))
            oh_ref[:, pl.ds(pl.multiple_of(s * 128, 128), 128)] = jnp.where(hit, 1.0, 0.0).astype(BF16)
            x = k_ref[s] * jnp.broadcast_to(wts_ref[pl.ds(stride * s + at_weight, 1), :], (CC, 128))
            x1 = x.astype(BF16)
            x2 = (x - x1.astype(F32)).astype(BF16)
            hib = jnp.broadcast_to(hi.astype(F32), (CC, 128)).astype(BF16)
            zero = jnp.zeros((CC, 128), BF16)
            for h in range(HI):
                m = hib == jnp.asarray(h, BF16)
                y_ref[2 * h * CC : (2 * h + 1) * CC, at] = jnp.where(m, x1, zero)
                y_ref[(2 * h + 1) * CC : (2 * h + 2) * CC, at] = jnp.where(m, x2, zero)

    def add(y_ref, i):
        oh = oh_ref[:, pl.ds(pl.multiple_of(i * CA * 128, CA * 128), CA * 128)]
        acc_ref[...] += lax.dot_general(
            y_ref[...], oh, (((1,), (1,)), ((), ())), preferred_element_type=F32
        )

    def add_two(t, carry):
        add(y0_ref, 2 * t)
        spread(y1_ref, 2 * t + 1)
        add(y1_ref, 2 * t + 1)
        spread(y0_ref, 2 * t + 2)
        return carry

    steps = SRC // CA
    spread(y0_ref, 0)
    lax.fori_loop(0, steps // 2 - 1, add_two, 0)
    add(y0_ref, steps - 2)
    spread(y1_ref, steps - 1)
    add(y1_ref, steps - 1)

    squares = jnp.zeros((8, 128), F32)
    beta_b = jnp.broadcast_to(beta, (CC, 128))
    if not first:
        back = jnp.broadcast_to(beta / aprev_ref[...], (CC, 128))
    for h in range(HI):
        for t in range(LO // 128):
            at = slice(t * 128, (t + 1) * 128)
            g = acc_ref[2 * h * CC : (2 * h + 1) * CC, at] + acc_ref[(2 * h + 1) * CC : (2 * h + 2) * CC, at]
            g = g / beta_b
            cols = slice(h * LO + t * 128, h * LO + (t + 1) * 128)
            if not first:
                g = g - pprev_ref[:, cols] * back
            p_ref[:, cols] = g
            g1 = g.astype(BF16)
            v_ref[h * CC : (h + 1) * CC, at] = g1
            v_ref[(HI + h) * CC : (HI + h + 1) * CC, at] = (g - g1.astype(F32)).astype(BF16)
            g2 = g * g
            squares = squares + g2[0:8] + g2[8:16] + g2[16:24] + g2[24:32]
    vals_ref[pl.ds(1, SRC, stride=2), :] = jnp.full((SRC, 128), jnp.sum(squares), F32)

    def fetch(g_ref, i):
        oh = oh_ref[:, pl.ds(pl.multiple_of(i * CF * 128, CF * 128), CF * 128)]
        g_ref[...] = lax.dot_general(v_ref[...], oh, (((1,), (0,)), ((), ())), preferred_element_type=F32)

    def use(g_ref, i):
        for c in range(CF):
            s = i * CF + c
            at = slice(c * 128, (c + 1) * 128)
            hi = jnp.broadcast_to(jnp.right_shift(ids_ref[pl.ds(s, 1), :], 8), (8, 128))
            ks = [k_ref[s, j : j + 8, :] for j in range(0, CC, 8)]
            total = jnp.zeros((8, 128), F32)
            for h in range(HI):
                part = None
                for j, kj in zip(range(0, CC, 8), ks):
                    r = h * CC + j
                    e = (g_ref[r : r + 8, at] + g_ref[HI * CC + r : HI * CC + r + 8, at]) * kj
                    part = e if part is None else part + e
                total = jnp.where(hi == h, part, total)
            vals_ref[pl.ds(2 * s, 1), :] = jnp.sum(total, axis=0, keepdims=True)

    def fetch_two(t, carry):
        fetch(g1_ref, 2 * t + 1)
        use(g0_ref, 2 * t)
        fetch(g0_ref, 2 * t + 2)
        use(g1_ref, 2 * t + 1)
        return carry

    steps = SRC // CF
    fetch(g0_ref, 0)
    lax.fori_loop(0, steps // 2 - 1, fetch_two, 0)
    fetch(g1_ref, steps - 1)
    use(g0_ref, steps - 2)
    use(g1_ref, steps - 1)


def owner_call(first, k, ids, weights, prev, alpha):
    outs = [
        jax.ShapeDtypeStruct((CC, BLK_DEV), F32),
        jax.ShapeDtypeStruct((2 * SRC, 128), F32),
        jax.ShapeDtypeStruct((1, 128), F32),
    ]
    if first:
        outs.append(jax.ShapeDtypeStruct((SRC, 128), jnp.int32))
    return pl.pallas_call(
        functools.partial(owner_kernel, first),
        out_shape=tuple(outs),
        scratch_shapes=[
            pltpu.VMEM((LO, SRC * 128), BF16),
            pltpu.VMEM((2 * HI * CC, CA * 128), BF16),
            pltpu.VMEM((2 * HI * CC, CA * 128), BF16),
            pltpu.VMEM((2 * HI * CC, LO), F32),
            pltpu.VMEM((2 * HI * CC, LO), BF16),
            pltpu.VMEM((2 * HI * CC, CF * 128), F32),
            pltpu.VMEM((2 * HI * CC, CF * 128), F32),
        ],
        compiler_params=pltpu.CompilerParams(vmem_limit_bytes=32 << 20),
        name="owner",
    )(k, ids, weights, prev, alpha)


def window_kernel(vals_ref, ray_ref, q_ref, beta_ref, wts_ref, qout_ref, alpha_ref, norm_ref, a_ref, b_ref):
    alpha = jnp.sqrt(jnp.sum(rows(vals_ref, 1, SRC, 2), axis=0, keepdims=True))
    alpha_ref[...] = alpha
    vals = rows(vals_ref, 0, N_WIN, 4) + rows(vals_ref, 2, N_WIN, 4)
    v1 = vals.astype(BF16).astype(F32)
    v2 = (vals - v1).astype(BF16).astype(F32)
    v3 = vals - v1 - v2
    ray = ray_ref[...]
    lo = jnp.bitwise_and(ray, 127)
    hi = jnp.right_shift(ray, 7)
    sub = lax.broadcasted_iota(jnp.int32, (8, 128), 0)
    tier = jnp.bitwise_and(sub, RT - 1)
    lo_iota = lax.broadcasted_iota(jnp.int32, (128, 128), 0)
    wide = lambda r, p, n: jnp.broadcast_to(r[p : p + 1], (n, 128))
    for p in range(N_WIN):
        at = slice(p * 128, (p + 1) * 128)
        hit = tier == wide(hi, p, 8)
        upper = jnp.where(sub < RT, wide(v1, p, 8), wide(v2, p, 8))
        lower = jnp.where(sub < RT, wide(v3, p, 8), 0.0)
        both = jnp.concatenate([jnp.where(hit, upper, 0.0), jnp.where(hit, lower, 0.0)], axis=0)
        a_ref[:, at] = both.astype(BF16)
        b_ref[:, at] = jnp.where(lo_iota == wide(lo, p, 128), 1.0, 0.0).astype(BF16)
    out = lax.dot_general(a_ref[...], b_ref[...], (((1,), (1,)), ((), ())), preferred_element_type=F32)
    summed = out[0:RT] + out[RT : 2 * RT] + out[2 * RT : 3 * RT]
    alpha_b = jnp.broadcast_to(alpha, (RT, 128))
    beta_b = jnp.broadcast_to(beta_ref[...], (RT, 128))
    q = summed / alpha_b - alpha_b * (q_ref[...] / beta_b)
    qout_ref[...] = q
    part = jnp.sum(q * q)
    gather_rays(q, ray, wts_ref, 2, 0)
    wts_ref[pl.ds(1, SRC, stride=2), :] = jnp.full((SRC, 128), part, F32)
    norm_ref[...] = jnp.full((SRC, 128), part, F32)


def window_call(vals, ray, q, beta):
    return pl.pallas_call(
        window_kernel,
        out_shape=(
            jax.ShapeDtypeStruct((2 * SRC, 128), F32),
            jax.ShapeDtypeStruct((RT, 128), F32),
            jax.ShapeDtypeStruct((1, 128), F32),
            jax.ShapeDtypeStruct((SRC, 128), F32),
        ),
        scratch_shapes=[
            pltpu.VMEM((16, N_WIN * 128), BF16),
            pltpu.VMEM((128, N_WIN * 128), BF16),
        ],
        compiler_params=pltpu.CompilerParams(vmem_limit_bytes=8 << 20),
        name="window",
    )(vals, ray, q, beta)


def end_kernel(norm_ref, q_ref, *refs):
    mine, theirs = refs[0:ITERS], refs[ITERS : 2 * ITERS]
    alphas = [r[...] for r in refs[2 * ITERS : 3 * ITERS]]
    betas = [r[...] for r in refs[3 * ITERS : 4 * ITERS]]
    update_ref, data_ref = refs[4 * ITERS :]
    betas.append(jnp.sqrt(jnp.sum(norm_ref[...], axis=0, keepdims=True)))
    data_ref[...] = q_ref[...] / jnp.broadcast_to(betas[ITERS], (RT, 128))
    one = jnp.ones_like(alphas[0])
    phibar, rhobar = betas[0], alphas[0]
    search = [one]
    update = [jnp.zeros_like(one) for _ in range(ITERS)]
    for step in range(ITERS):
        beta = betas[step + 1]
        rho = jnp.sqrt(rhobar * rhobar + beta * beta)
        cosine = rhobar / rho
        sine = beta / rho
        phi = cosine * phibar
        phibar = sine * phibar
        for i, s in enumerate(search):
            update[i] = update[i] + phi / rho * s
        if step + 1 < ITERS:
            theta = sine * alphas[step + 1]
            rhobar = -cosine * alphas[step + 1]
            search = [-(theta / rho * s) for s in search] + [one]
    scale = [jnp.broadcast_to(u / a, (CC, 128)) for u, a in zip(update, alphas)]
    core = lax.axis_index("off")
    for refs_in, half in ((mine, core), (theirs, 1 - core)):
        at = pl.ds(pl.multiple_of(half * CC, CC), CC)
        for t in range(BLK_DEV // 128):
            cols = slice(t * 128, (t + 1) * 128)
            total = refs_in[0][:, cols] * scale[0]
            for i in range(1, ITERS):
                total = total + refs_in[i][:, cols] * scale[i]
            update_ref[at, cols] = total


def end_call(norm, q, mine, theirs, alphas, betas):
    return pl.pallas_call(
        end_kernel,
        out_shape=(
            jax.ShapeDtypeStruct((CELLS, BLK_DEV), F32),
            jax.ShapeDtypeStruct((RT, 128), F32),
        ),
        compiler_params=pltpu.CompilerParams(vmem_limit_bytes=8 << 20),
        name="end",
    )(norm, q, *mine, *theirs, *alphas, *betas)


def exchange(x):
    rest = x.shape[0] // SRC
    y = lax.all_to_all(x.reshape(SRC, rest, 128), ("win", "off"), 0, 0, tiled=True)
    return y.reshape(x.shape)


def body(kernels, blocks, counts, ray_of, slopes):
    ray = ray_of.reshape(N_WIN, CAP)
    q = slopes.reshape(RT, 128)
    k = lax.all_to_all(kernels.reshape(SRC, CC, CAP), ("win", "off"), 0, 0, tiled=True)
    weights = exchange(start_call(blocks.reshape(N_WIN, CAP), counts.reshape(1, N_WIN), ray, q))
    ids = weights
    prev, alpha = jnp.zeros((8, 128), F32), jnp.zeros((1, 128), F32)
    mine, theirs, alphas, betas = [], [], [], []
    for step in range(ITERS):
        prev, vals, beta, *rest = owner_call(step == 0, k, ids, weights, prev, alpha)
        ids = rest[0] if rest else ids
        mine.append(prev)
        theirs.append(lax.ppermute(prev, "off", [(0, 1), (1, 0)]))
        betas.append(beta)
        weights, q, alpha, norm = window_call(exchange(vals), ray, q, beta)
        alphas.append(alpha)
        weights = exchange(weights)
    owner_call(False, k, ids, weights, prev, alpha)
    update, data = end_call(exchange(norm), q, mine, theirs, alphas, betas)
    return update, data.reshape(1, 1, RAYS)


def solution(mesh):
    in_specs = (
        P("off", "win", None, None, None),
        P("off", "win", None, None),
        P("off", "win", None),
        P("off", "win", None, None),
        P("off", "win", None),
    )
    out_specs = (P(None, "win"), P("off", "win", None))
    return jax.shard_map(body, mesh=mesh, in_specs=in_specs, out_specs=out_specs, check_vma=False)
```

```python
import functools

import jax
import jax.numpy as jnp
from jax import lax
from jax.experimental import pallas as pl
from jax.experimental.pallas import tpu as pltpu
from jax.sharding import PartitionSpec as P

CELLS = 64
CAP = 128
BLK_DEV = 2048
RAYS = 512
ITERS = 3
N_OFF = 2
N_WIN = 64
SRC = N_OFF * N_WIN
CC = CELLS // N_OFF
RT = RAYS // 128
HI = 8
LO = BLK_DEV // HI
CA = 16
CF = 8
SLAB = CC + 8
F32 = jnp.float32
BF16 = jnp.bfloat16


def rows(ref, start, count, stride):
    return ref[pl.ds(start, count, stride=stride), :]


def gather_rays(data, ray, out_ref, first, half, whole):
    lo = jnp.bitwise_and(ray, 127)
    hi = jnp.right_shift(ray, 7)
    parts = []
    for g in range(N_WIN // 8):
        lo_g, hi_g = lo[g * 8 : g * 8 + 8], hi[g * 8 : g * 8 + 8]
        acc = jnp.zeros((8, 128), F32)
        for t in range(RT):
            table = jnp.broadcast_to(data[t : t + 1], (8, 128))
            got = jnp.take_along_axis(table, lo_g, axis=1, mode="promise_in_bounds")
            acc = jnp.where(hi_g == t, got, acc)
        parts.append(acc)
    weights = jnp.concatenate(parts, axis=0)
    out_ref[pl.ds(first, N_WIN, stride=whole), :] = weights
    out_ref[pl.ds(first + half, N_WIN, stride=whole), :] = weights


def start_kernel(k_ref, blocks_in, counts_in, ray_in, slopes_in, out_ref, *scratch):
    blocks_ref, counts_ref, ray_ref, slopes_ref, extra_ref, sems = scratch
    rows_out = pltpu.make_async_copy(k_ref, out_ref.at[:, 0:CC, :], sems.at[0])
    rows_out.start()
    loads = [
        pltpu.make_async_copy(src, dst, sems.at[2 + n])
        for n, (src, dst) in enumerate(
            ((blocks_in, blocks_ref), (counts_in, counts_ref), (ray_in, ray_ref), (slopes_in, slopes_ref))
        )
    ]
    for load in loads:
        load.start()
    for load in loads:
        load.wait()
    slot = lax.broadcasted_iota(jnp.int32, (N_WIN, CAP), 1)
    row = lax.broadcasted_iota(jnp.int32, (N_WIN, N_WIN), 0)
    col = lax.broadcasted_iota(jnp.int32, (N_WIN, N_WIN), 1)
    counts = jnp.broadcast_to(counts_ref[...].astype(F32), (N_WIN, N_WIN))
    counts = jnp.sum(jnp.where(row == col, counts, 0.0), axis=1, keepdims=True)
    ids = jnp.where(slot.astype(F32) < counts, blocks_ref[...].astype(F32), -1.0)
    extra_ref[...] = jnp.zeros_like(extra_ref)
    extra_ref[pl.ds(0, N_WIN, stride=16), :] = ids
    extra_ref[pl.ds(8, N_WIN, stride=16), :] = ids
    data = slopes_ref[...]
    gather_rays(data, ray_ref[...], extra_ref, 1, 8, 16)
    extra_ref[pl.ds(2, SRC, stride=8), :] = jnp.full((SRC, 128), jnp.sum(data * data), F32)
    extra_out = pltpu.make_async_copy(
        extra_ref.reshape(SRC, 8, 128), out_ref.at[:, CC:SLAB, :], sems.at[1]
    )
    extra_out.start()
    rows_out.wait()
    extra_out.wait()


def start_call(k, blocks, counts, ray, slopes):
    return pl.pallas_call(
        start_kernel,
        out_shape=jax.ShapeDtypeStruct((SRC, SLAB, 128), F32),
        in_specs=[pl.BlockSpec(memory_space=pltpu.HBM)] * 5,
        out_specs=pl.BlockSpec(memory_space=pltpu.HBM),
        scratch_shapes=[
            pltpu.VMEM((N_WIN, CAP), jnp.int32),
            pltpu.VMEM((1, N_WIN), jnp.int32),
            pltpu.VMEM((N_WIN, CAP), jnp.int32),
            pltpu.VMEM((RT, 128), F32),
            pltpu.VMEM((8 * SRC, 128), F32),
            pltpu.SemaphoreType.DMA((6,)),
        ],
        compiler_params=pltpu.CompilerParams(vmem_limit_bytes=4 << 20),
        name="start",
    )(k, blocks, counts, ray, slopes)


def owner_kernel(first, k_ref, *refs):
    if first:
        p_ref, vals_ref, beta_ref, ids_ref, *scratch = refs
        ids_ref[...] = k_ref[:, CC, :].astype(jnp.int32)
        norms = k_ref[:, CC + 2, :]
        weight_of = lambda s: k_ref[s, CC + 1 : CC + 2, :]
    else:
        ids_ref, wts_ref, pprev_ref, aprev_ref, p_ref, vals_ref, beta_ref, *scratch = refs
        norms = rows(wts_ref, 1, SRC, 2)
        weight_of = lambda s: wts_ref[pl.ds(2 * s, 1), :]
    oh_ref, y0_ref, y1_ref, acc_ref, v_ref, g0_ref, g1_ref = scratch
    beta = jnp.sqrt(jnp.sum(norms, axis=0, keepdims=True))
    beta_ref[...] = beta
    acc_ref[...] = jnp.zeros_like(acc_ref)
    lo_iota = lax.broadcasted_iota(jnp.int32, (LO, 128), 0)

    def spread(y_ref, i):
        for c in range(CA):
            s = i * CA + c
            at = slice(c * 128, (c + 1) * 128)
            blk = ids_ref[pl.ds(s, 1), :]
            lo = jnp.where(blk < 0, -1, jnp.bitwise_and(blk, LO - 1))
            hi = jnp.right_shift(blk, 8)
            hit = lo_iota == jnp.broadcast_to(lo, (LO, 128))
            oh_ref[:, pl.ds(pl.multiple_of(s * 128, 128), 128)] = jnp.where(hit, 1.0, 0.0).astype(BF16)
            x = k_ref[s, 0:CC, :] * jnp.broadcast_to(weight_of(s), (CC, 128))
            x1 = x.astype(BF16)
            x2 = (x - x1.astype(F32)).astype(BF16)
            hib = jnp.broadcast_to(hi.astype(F32), (CC, 128)).astype(BF16)
            zero = jnp.zeros((CC, 128), BF16)
            for h in range(HI):
                m = hib == jnp.asarray(h, BF16)
                y_ref[2 * h * CC : (2 * h + 1) * CC, at] = jnp.where(m, x1, zero)
                y_ref[(2 * h + 1) * CC : (2 * h + 2) * CC, at] = jnp.where(m, x2, zero)

    def add(y_ref, i):
        oh = oh_ref[:, pl.ds(pl.multiple_of(i * CA * 128, CA * 128), CA * 128)]
        acc_ref[...] += lax.dot_general(
            y_ref[...], oh, (((1,), (1,)), ((), ())), preferred_element_type=F32
        )

    def add_two(t, carry):
        add(y0_ref, 2 * t)
        spread(y1_ref, 2 * t + 1)
        add(y1_ref, 2 * t + 1)
        spread(y0_ref, 2 * t + 2)
        return carry

    steps = SRC // CA
    spread(y0_ref, 0)
    lax.fori_loop(0, steps // 2 - 1, add_two, 0)
    add(y0_ref, steps - 2)
    spread(y1_ref, steps - 1)
    add(y1_ref, steps - 1)

    squares = jnp.zeros((8, 128), F32)
    beta_b = jnp.broadcast_to(beta, (CC, 128))
    if not first:
        back = jnp.broadcast_to(beta / aprev_ref[...], (CC, 128))
    for h in range(HI):
        for t in range(LO // 128):
            at = slice(t * 128, (t + 1) * 128)
            g = acc_ref[2 * h * CC : (2 * h + 1) * CC, at] + acc_ref[(2 * h + 1) * CC : (2 * h + 2) * CC, at]
            g = g / beta_b
            cols = slice(h * LO + t * 128, h * LO + (t + 1) * 128)
            if not first:
                g = g - pprev_ref[:, cols] * back
            p_ref[:, cols] = g
            g1 = g.astype(BF16)
            v_ref[h * CC : (h + 1) * CC, at] = g1
            v_ref[(HI + h) * CC : (HI + h + 1) * CC, at] = (g - g1.astype(F32)).astype(BF16)
            g2 = g * g
            squares = squares + g2[0:8] + g2[8:16] + g2[16:24] + g2[24:32]
    vals_ref[pl.ds(1, SRC, stride=2), :] = jnp.full((SRC, 128), jnp.sum(squares), F32)

    def fetch(g_ref, i):
        oh = oh_ref[:, pl.ds(pl.multiple_of(i * CF * 128, CF * 128), CF * 128)]
        g_ref[...] = lax.dot_general(v_ref[...], oh, (((1,), (0,)), ((), ())), preferred_element_type=F32)

    def use(g_ref, i):
        for c in range(CF):
            s = i * CF + c
            at = slice(c * 128, (c + 1) * 128)
            hi = jnp.broadcast_to(jnp.right_shift(ids_ref[pl.ds(s, 1), :], 8), (8, 128))
            ks = [k_ref[s, j : j + 8, :] for j in range(0, CC, 8)]
            total = jnp.zeros((8, 128), F32)
            for h in range(HI):
                part = None
                for j, kj in zip(range(0, CC, 8), ks):
                    r = h * CC + j
                    e = (g_ref[r : r + 8, at] + g_ref[HI * CC + r : HI * CC + r + 8, at]) * kj
                    part = e if part is None else part + e
                total = jnp.where(hi == h, part, total)
            vals_ref[pl.ds(2 * s, 1), :] = jnp.sum(total, axis=0, keepdims=True)

    def fetch_two(t, carry):
        fetch(g1_ref, 2 * t + 1)
        use(g0_ref, 2 * t)
        fetch(g0_ref, 2 * t + 2)
        use(g1_ref, 2 * t + 1)
        return carry

    steps = SRC // CF
    fetch(g0_ref, 0)
    lax.fori_loop(0, steps // 2 - 1, fetch_two, 0)
    fetch(g1_ref, steps - 1)
    use(g0_ref, steps - 2)
    use(g1_ref, steps - 1)


def owner_call(first, *args):
    outs = [
        jax.ShapeDtypeStruct((CC, BLK_DEV), F32),
        jax.ShapeDtypeStruct((2 * SRC, 128), F32),
        jax.ShapeDtypeStruct((1, 128), F32),
    ]
    if first:
        outs.append(jax.ShapeDtypeStruct((SRC, 128), jnp.int32))
    return pl.pallas_call(
        functools.partial(owner_kernel, first),
        out_shape=tuple(outs),
        scratch_shapes=[
            pltpu.VMEM((LO, SRC * 128), BF16),
            pltpu.VMEM((2 * HI * CC, CA * 128), BF16),
            pltpu.VMEM((2 * HI * CC, CA * 128), BF16),
            pltpu.VMEM((2 * HI * CC, LO), F32),
            pltpu.VMEM((2 * HI * CC, LO), BF16),
            pltpu.VMEM((2 * HI * CC, CF * 128), F32),
            pltpu.VMEM((2 * HI * CC, CF * 128), F32),
        ],
        compiler_params=pltpu.CompilerParams(vmem_limit_bytes=32 << 20),
        name="owner",
    )(*args)


def window_kernel(vals_ref, ray_ref, q_ref, beta_ref, wts_ref, qout_ref, alpha_ref, norm_ref, a_ref, b_ref):
    alpha = jnp.sqrt(jnp.sum(rows(vals_ref, 1, SRC, 2), axis=0, keepdims=True))
    alpha_ref[...] = alpha
    vals = rows(vals_ref, 0, N_WIN, 4) + rows(vals_ref, 2, N_WIN, 4)
    v1 = vals.astype(BF16).astype(F32)
    v2 = (vals - v1).astype(BF16).astype(F32)
    v3 = vals - v1 - v2
    ray = ray_ref[...]
    lo = jnp.bitwise_and(ray, 127)
    hi = jnp.right_shift(ray, 7)
    sub = lax.broadcasted_iota(jnp.int32, (8, 128), 0)
    tier = jnp.bitwise_and(sub, RT - 1)
    lo_iota = lax.broadcasted_iota(jnp.int32, (128, 128), 0)
    wide = lambda r, p, n: jnp.broadcast_to(r[p : p + 1], (n, 128))
    for p in range(N_WIN):
        at = slice(p * 128, (p + 1) * 128)
        hit = tier == wide(hi, p, 8)
        upper = jnp.where(sub < RT, wide(v1, p, 8), wide(v2, p, 8))
        lower = jnp.where(sub < RT, wide(v3, p, 8), 0.0)
        both = jnp.concatenate([jnp.where(hit, upper, 0.0), jnp.where(hit, lower, 0.0)], axis=0)
        a_ref[:, at] = both.astype(BF16)
        b_ref[:, at] = jnp.where(lo_iota == wide(lo, p, 128), 1.0, 0.0).astype(BF16)
    out = lax.dot_general(a_ref[...], b_ref[...], (((1,), (1,)), ((), ())), preferred_element_type=F32)
    summed = out[0:RT] + out[RT : 2 * RT] + out[2 * RT : 3 * RT]
    alpha_b = jnp.broadcast_to(alpha, (RT, 128))
    beta_b = jnp.broadcast_to(beta_ref[...], (RT, 128))
    q = summed / alpha_b - alpha_b * (q_ref[...] / beta_b)
    qout_ref[...] = q
    part = jnp.sum(q * q)
    gather_rays(q, ray, wts_ref, 0, 2, 4)
    wts_ref[pl.ds(1, SRC, stride=2), :] = jnp.full((SRC, 128), part, F32)
    norm_ref[...] = jnp.full((SRC, 128), part, F32)


def window_call(vals, ray, q, beta):
    return pl.pallas_call(
        window_kernel,
        out_shape=(
            jax.ShapeDtypeStruct((2 * SRC, 128), F32),
            jax.ShapeDtypeStruct((RT, 128), F32),
            jax.ShapeDtypeStruct((1, 128), F32),
            jax.ShapeDtypeStruct((SRC, 128), F32),
        ),
        scratch_shapes=[
            pltpu.VMEM((16, N_WIN * 128), BF16),
            pltpu.VMEM((128, N_WIN * 128), BF16),
        ],
        compiler_params=pltpu.CompilerParams(vmem_limit_bytes=8 << 20),
        name="window",
    )(vals, ray, q, beta)


def end_kernel(norm_ref, q_ref, *refs):
    mine, theirs = refs[0:ITERS], refs[ITERS : 2 * ITERS]
    alphas = [r[...] for r in refs[2 * ITERS : 3 * ITERS]]
    betas = [r[...] for r in refs[3 * ITERS : 4 * ITERS]]
    update_ref, data_ref = refs[4 * ITERS :]
    betas.append(jnp.sqrt(jnp.sum(norm_ref[...], axis=0, keepdims=True)))
    data_ref[...] = q_ref[...] / jnp.broadcast_to(betas[ITERS], (RT, 128))
    one = jnp.ones_like(alphas[0])
    phibar, rhobar = betas[0], alphas[0]
    search = [one]
    update = [jnp.zeros_like(one) for _ in range(ITERS)]
    for step in range(ITERS):
        beta = betas[step + 1]
        rho = jnp.sqrt(rhobar * rhobar + beta * beta)
        cosine = rhobar / rho
        sine = beta / rho
        phi = cosine * phibar
        phibar = sine * phibar
        for i, s in enumerate(search):
            update[i] = update[i] + phi / rho * s
        if step + 1 < ITERS:
            theta = sine * alphas[step + 1]
            rhobar = -cosine * alphas[step + 1]
            search = [-(theta / rho * s) for s in search] + [one]
    scale = [jnp.broadcast_to(u / a, (CC, 128)) for u, a in zip(update, alphas)]
    core = lax.axis_index("off")
    for refs_in, half in ((mine, core), (theirs, 1 - core)):
        at = pl.ds(pl.multiple_of(half * CC, CC), CC)
        for t in range(BLK_DEV // 128):
            cols = slice(t * 128, (t + 1) * 128)
            total = refs_in[0][:, cols] * scale[0]
            for i in range(1, ITERS):
                total = total + refs_in[i][:, cols] * scale[i]
            update_ref[at, cols] = total


def end_call(norm, q, mine, theirs, alphas, betas):
    return pl.pallas_call(
        end_kernel,
        out_shape=(
            jax.ShapeDtypeStruct((CELLS, BLK_DEV), F32),
            jax.ShapeDtypeStruct((RT, 128), F32),
        ),
        compiler_params=pltpu.CompilerParams(vmem_limit_bytes=8 << 20),
        name="end",
    )(norm, q, *mine, *theirs, *alphas, *betas)


def exchange(x):
    rest = x.shape[0] // SRC
    y = lax.all_to_all(x.reshape(SRC, rest, 128), ("win", "off"), 0, 0, tiled=True)
    return y.reshape(x.shape)


def body(kernels, blocks, counts, ray_of, slopes):
    ray = ray_of.reshape(N_WIN, CAP)
    q = slopes.reshape(RT, 128)
    k = start_call(
        kernels.reshape(SRC, CC, CAP), blocks.reshape(N_WIN, CAP), counts.reshape(1, N_WIN), ray, q
    )
    k = lax.all_to_all(k, ("win", "off"), 0, 0, tiled=True)
    mine, theirs, alphas, betas = [], [], [], []
    for step in range(ITERS):
        if step == 0:
            prev, vals, beta, ids = owner_call(True, k)
        else:
            prev, vals, beta = owner_call(False, k, ids, weights, prev, alpha)
        mine.append(prev)
        theirs.append(lax.ppermute(prev, "off", [(0, 1), (1, 0)]))
        betas.append(beta)
        weights, q, alpha, norm = window_call(exchange(vals), ray, q, beta)
        alphas.append(alpha)
        weights = exchange(weights)
    owner_call(False, k, ids, weights, prev, alpha)
    update, data = end_call(exchange(norm), q, mine, theirs, alphas, betas)
    return update, data.reshape(1, 1, RAYS)


def solution(mesh):
    in_specs = (
        P("off", "win", None, None, None),
        P("off", "win", None, None),
        P("off", "win", None),
        P("off", "win", None, None),
        P("off", "win", None),
    )
    out_specs = (P(None, "win"), P("off", "win", None))
    return jax.shard_map(body, mesh=mesh, in_specs=in_specs, out_specs=out_specs, check_vma=False)
```

```python
import functools

import jax
import jax.numpy as jnp
from jax import lax
from jax.experimental import pallas as pl
from jax.experimental.pallas import tpu as pltpu
from jax.sharding import PartitionSpec as P

CELLS = 64
CAP = 128
BLK_DEV = 2048
RAYS = 512
ITERS = 3
N_OFF = 2
N_WIN = 64
SRC = N_OFF * N_WIN
CC = CELLS // N_OFF
RT = RAYS // 128
HI = 8
LO = BLK_DEV // HI
CA = 16
CF = 8
SLAB = CC + 8
F32 = jnp.float32
BF16 = jnp.bfloat16


def rows(ref, start, count, stride):
    return ref[pl.ds(start, count, stride=stride), :]


def gather_rays(data, ray, out_ref, first, half, whole):
    lo = jnp.bitwise_and(ray, 127)
    hi = jnp.right_shift(ray, 7)
    parts = []
    for g in range(N_WIN // 8):
        lo_g, hi_g = lo[g * 8 : g * 8 + 8], hi[g * 8 : g * 8 + 8]
        acc = jnp.zeros((8, 128), F32)
        for t in range(RT):
            table = jnp.broadcast_to(data[t : t + 1], (8, 128))
            got = jnp.take_along_axis(table, lo_g, axis=1, mode="promise_in_bounds")
            acc = jnp.where(hi_g == t, got, acc)
        parts.append(acc)
    weights = jnp.concatenate(parts, axis=0)
    out_ref[pl.ds(first, N_WIN, stride=whole), :] = weights
    out_ref[pl.ds(first + half, N_WIN, stride=whole), :] = weights


def start_kernel(k_ref, blocks_in, counts_in, ray_in, slopes_in, out_ref, *scratch):
    blocks_ref, counts_ref, ray_ref, slopes_ref, extra_ref, sems = scratch
    rows_out = pltpu.make_async_copy(k_ref, out_ref.at[:, 0:CC, :], sems.at[0])
    rows_out.start()
    loads = [
        pltpu.make_async_copy(src, dst, sems.at[2 + n])
        for n, (src, dst) in enumerate(
            ((blocks_in, blocks_ref), (counts_in, counts_ref), (ray_in, ray_ref), (slopes_in, slopes_ref))
        )
    ]
    for load in loads:
        load.start()
    for load in loads:
        load.wait()
    slot = lax.broadcasted_iota(jnp.int32, (N_WIN, CAP), 1)
    row = lax.broadcasted_iota(jnp.int32, (N_WIN, N_WIN), 0)
    col = lax.broadcasted_iota(jnp.int32, (N_WIN, N_WIN), 1)
    counts = jnp.broadcast_to(counts_ref[...].astype(F32), (N_WIN, N_WIN))
    counts = jnp.sum(jnp.where(row == col, counts, 0.0), axis=1, keepdims=True)
    ids = jnp.where(slot.astype(F32) < counts, blocks_ref[...].astype(F32), -1.0)
    extra_ref[...] = jnp.zeros_like(extra_ref)
    extra_ref[pl.ds(0, N_WIN, stride=16), :] = ids
    extra_ref[pl.ds(8, N_WIN, stride=16), :] = ids
    data = slopes_ref[...]
    gather_rays(data, ray_ref[...], extra_ref, 1, 8, 16)
    extra_ref[pl.ds(2, SRC, stride=8), :] = jnp.full((SRC, 128), jnp.sum(data * data), F32)
    extra_out = pltpu.make_async_copy(
        extra_ref.reshape(SRC, 8, 128), out_ref.at[:, CC:SLAB, :], sems.at[1]
    )
    extra_out.start()
    rows_out.wait()
    extra_out.wait()


def start_call(k, blocks, counts, ray, slopes):
    return pl.pallas_call(
        start_kernel,
        out_shape=jax.ShapeDtypeStruct((SRC, SLAB, 128), F32),
        in_specs=[pl.BlockSpec(memory_space=pltpu.HBM)] * 5,
        out_specs=pl.BlockSpec(memory_space=pltpu.HBM),
        scratch_shapes=[
            pltpu.VMEM((N_WIN, CAP), jnp.int32),
            pltpu.VMEM((1, N_WIN), jnp.int32),
            pltpu.VMEM((N_WIN, CAP), jnp.int32),
            pltpu.VMEM((RT, 128), F32),
            pltpu.VMEM((8 * SRC, 128), F32),
            pltpu.SemaphoreType.DMA((6,)),
        ],
        compiler_params=pltpu.CompilerParams(vmem_limit_bytes=4 << 20),
        name="start",
    )(*(pltpu.with_memory_space_constraint(x, pltpu.HBM) for x in (k, blocks, counts, ray, slopes)))


def owner_kernel(first, k_ref, *refs):
    if first:
        p_ref, vals_ref, beta_ref, ids_ref, oh_hbm, *scratch = refs
        ids_ref[...] = k_ref[:, CC, :].astype(jnp.int32)
        norms = k_ref[:, CC + 2, :]
        weight_of = lambda s: k_ref[s, CC + 1 : CC + 2, :]
    else:
        oh_hbm, ids_ref, wts_ref, pprev_ref, aprev_ref, p_ref, vals_ref, beta_ref, *scratch = refs
        norms = rows(wts_ref, 1, SRC, 2)
        weight_of = lambda s: wts_ref[pl.ds(2 * s, 1), :]
    oh_ref, y0_ref, y1_ref, acc_ref, v_ref, g0_ref, g1_ref, sems = scratch
    steps = SRC // CA

    def kept(i):
        at = pl.ds(pl.multiple_of(i * CA * 128, CA * 128), CA * 128)
        ends = (oh_ref.at[:, at], oh_hbm.at[:, at])
        return pltpu.make_async_copy(*(ends if first else ends[::-1]), sems.at[i])

    if not first:
        for i in range(steps):
            kept(i).start()
    beta = jnp.sqrt(jnp.sum(norms, axis=0, keepdims=True))
    beta_ref[...] = beta
    acc_ref[...] = jnp.zeros_like(acc_ref)
    lo_iota = lax.broadcasted_iota(jnp.int32, (LO, 128), 0).astype(F32).astype(BF16)

    def spread(y_ref, i):
        for c in range(CA):
            s = i * CA + c
            at = slice(c * 128, (c + 1) * 128)
            blk = ids_ref[pl.ds(s, 1), :]
            hi = jnp.right_shift(blk, 8)
            if first:
                lo = jnp.where(blk < 0, -1, jnp.bitwise_and(blk, LO - 1)).astype(F32)
                hit = lo_iota == jnp.broadcast_to(lo, (LO, 128)).astype(BF16)
                oh_ref[:, pl.ds(pl.multiple_of(s * 128, 128), 128)] = jnp.where(
                    hit, jnp.ones((LO, 128), BF16), jnp.zeros((LO, 128), BF16)
                )
            x = k_ref[s, 0:CC, :] * jnp.broadcast_to(weight_of(s), (CC, 128))
            x1 = x.astype(BF16)
            x2 = (x - x1.astype(F32)).astype(BF16)
            hib = jnp.broadcast_to(hi.astype(F32), (CC, 128)).astype(BF16)
            zero = jnp.zeros((CC, 128), BF16)
            for h in range(HI):
                m = hib == jnp.asarray(h, BF16)
                y_ref[2 * h * CC : (2 * h + 1) * CC, at] = jnp.where(m, x1, zero)
                y_ref[(2 * h + 1) * CC : (2 * h + 2) * CC, at] = jnp.where(m, x2, zero)

    def add(y_ref, i):
        if not first:
            kept(i).wait()
        oh = oh_ref[:, pl.ds(pl.multiple_of(i * CA * 128, CA * 128), CA * 128)]
        acc_ref[...] += lax.dot_general(
            y_ref[...], oh, (((1,), (1,)), ((), ())), preferred_element_type=F32
        )

    def add_two(t, carry):
        add(y0_ref, 2 * t)
        spread(y1_ref, 2 * t + 1)
        add(y1_ref, 2 * t + 1)
        spread(y0_ref, 2 * t + 2)
        return carry

    spread(y0_ref, 0)
    lax.fori_loop(0, steps // 2 - 1, add_two, 0)
    add(y0_ref, steps - 2)
    spread(y1_ref, steps - 1)
    add(y1_ref, steps - 1)

    if first:
        for i in range(steps):
            kept(i).start()
    squares = jnp.zeros((8, 128), F32)
    beta_b = jnp.broadcast_to(beta, (CC, 128))
    if not first:
        back = jnp.broadcast_to(beta / aprev_ref[...], (CC, 128))
    for h in range(HI):
        for t in range(LO // 128):
            at = slice(t * 128, (t + 1) * 128)
            g = acc_ref[2 * h * CC : (2 * h + 1) * CC, at] + acc_ref[(2 * h + 1) * CC : (2 * h + 2) * CC, at]
            g = g / beta_b
            cols = slice(h * LO + t * 128, h * LO + (t + 1) * 128)
            if not first:
                g = g - pprev_ref[:, cols] * back
            p_ref[:, cols] = g
            g1 = g.astype(BF16)
            v_ref[h * CC : (h + 1) * CC, at] = g1
            v_ref[(HI + h) * CC : (HI + h + 1) * CC, at] = (g - g1.astype(F32)).astype(BF16)
            g2 = g * g
            squares = squares + g2[0:8] + g2[8:16] + g2[16:24] + g2[24:32]
    vals_ref[pl.ds(1, SRC, stride=2), :] = jnp.full((SRC, 128), jnp.sum(squares), F32)

    def fetch(g_ref, i):
        oh = oh_ref[:, pl.ds(pl.multiple_of(i * CF * 128, CF * 128), CF * 128)]
        g_ref[...] = lax.dot_general(v_ref[...], oh, (((1,), (0,)), ((), ())), preferred_element_type=F32)

    def use(g_ref, i):
        for c in range(CF):
            s = i * CF + c
            at = slice(c * 128, (c + 1) * 128)
            hi = jnp.broadcast_to(jnp.right_shift(ids_ref[pl.ds(s, 1), :], 8), (8, 128))
            ks = [k_ref[s, j : j + 8, :] for j in range(0, CC, 8)]
            total = jnp.zeros((8, 128), F32)
            for h in range(HI):
                part = None
                for j, kj in zip(range(0, CC, 8), ks):
                    r = h * CC + j
                    e = (g_ref[r : r + 8, at] + g_ref[HI * CC + r : HI * CC + r + 8, at]) * kj
                    part = e if part is None else part + e
                total = jnp.where(hi == h, part, total)
            vals_ref[pl.ds(2 * s, 1), :] = jnp.sum(total, axis=0, keepdims=True)

    def fetch_two(t, carry):
        fetch(g1_ref, 2 * t + 1)
        use(g0_ref, 2 * t)
        fetch(g0_ref, 2 * t + 2)
        use(g1_ref, 2 * t + 1)
        return carry

    last = SRC // CF - 1
    fetch(g0_ref, 0)
    lax.fori_loop(0, last // 2, fetch_two, 0)
    fetch(g1_ref, last)
    use(g0_ref, last - 1)
    use(g1_ref, last)
    if first:
        for i in range(steps):
            kept(i).wait()


def owner_call(first, *args):
    outs = [
        jax.ShapeDtypeStruct((CC, BLK_DEV), F32),
        jax.ShapeDtypeStruct((2 * SRC, 128), F32),
        jax.ShapeDtypeStruct((1, 128), F32),
    ]
    vmem, hbm = pl.BlockSpec(memory_space=pltpu.VMEM), pl.BlockSpec(memory_space=pltpu.HBM)
    in_specs, out_specs = [vmem] * len(args), [vmem] * 3
    if first:
        outs.append(jax.ShapeDtypeStruct((SRC, 128), jnp.int32))
        outs.append(pltpu.HBM((LO, SRC * 128), BF16))
        out_specs += [vmem, hbm]
    else:
        in_specs[1] = hbm
        args = (args[0], pltpu.with_memory_space_constraint(args[1], pltpu.HBM), *args[2:])
    return pl.pallas_call(
        functools.partial(owner_kernel, first),
        out_shape=tuple(outs),
        in_specs=in_specs,
        out_specs=tuple(out_specs),
        scratch_shapes=[
            pltpu.VMEM((LO, SRC * 128), BF16),
            pltpu.VMEM((2 * HI * CC, CA * 128), BF16),
            pltpu.VMEM((2 * HI * CC, CA * 128), BF16),
            pltpu.VMEM((2 * HI * CC, LO), F32),
            pltpu.VMEM((2 * HI * CC, LO), BF16),
            pltpu.VMEM((2 * HI * CC, CF * 128), F32),
            pltpu.VMEM((2 * HI * CC, CF * 128), F32),
            pltpu.SemaphoreType.DMA((SRC // CA,)),
        ],
        compiler_params=pltpu.CompilerParams(vmem_limit_bytes=32 << 20),
        name="owner",
    )(*args)


def window_kernel(vals_ref, ray_ref, q_ref, beta_ref, wts_ref, qout_ref, alpha_ref, norm_ref, a_ref, b_ref):
    alpha = jnp.sqrt(jnp.sum(rows(vals_ref, 1, SRC, 2), axis=0, keepdims=True))
    alpha_ref[...] = alpha
    vals = rows(vals_ref, 0, N_WIN, 4) + rows(vals_ref, 2, N_WIN, 4)
    v1 = vals.astype(BF16).astype(F32)
    v2 = (vals - v1).astype(BF16).astype(F32)
    v3 = vals - v1 - v2
    ray = ray_ref[...]
    lo = jnp.bitwise_and(ray, 127)
    hi = jnp.right_shift(ray, 7)
    sub = lax.broadcasted_iota(jnp.int32, (8, 128), 0)
    tier = jnp.bitwise_and(sub, RT - 1)
    lo_iota = lax.broadcasted_iota(jnp.int32, (128, 128), 0)
    wide = lambda r, p, n: jnp.broadcast_to(r[p : p + 1], (n, 128))
    for p in range(N_WIN):
        at = slice(p * 128, (p + 1) * 128)
        hit = tier == wide(hi, p, 8)
        upper = jnp.where(sub < RT, wide(v1, p, 8), wide(v2, p, 8))
        lower = jnp.where(sub < RT, wide(v3, p, 8), 0.0)
        both = jnp.concatenate([jnp.where(hit, upper, 0.0), jnp.where(hit, lower, 0.0)], axis=0)
        a_ref[:, at] = both.astype(BF16)
        b_ref[:, at] = jnp.where(lo_iota == wide(lo, p, 128), 1.0, 0.0).astype(BF16)
    out = lax.dot_general(a_ref[...], b_ref[...], (((1,), (1,)), ((), ())), preferred_element_type=F32)
    summed = out[0:RT] + out[RT : 2 * RT] + out[2 * RT : 3 * RT]
    alpha_b = jnp.broadcast_to(alpha, (RT, 128))
    beta_b = jnp.broadcast_to(beta_ref[...], (RT, 128))
    q = summed / alpha_b - alpha_b * (q_ref[...] / beta_b)
    qout_ref[...] = q
    part = jnp.sum(q * q)
    gather_rays(q, ray, wts_ref, 0, 2, 4)
    wts_ref[pl.ds(1, SRC, stride=2), :] = jnp.full((SRC, 128), part, F32)
    norm_ref[...] = jnp.full((SRC, 128), part, F32)


def window_call(vals, ray, q, beta):
    return pl.pallas_call(
        window_kernel,
        out_shape=(
            jax.ShapeDtypeStruct((2 * SRC, 128), F32),
            jax.ShapeDtypeStruct((RT, 128), F32),
            jax.ShapeDtypeStruct((1, 128), F32),
            jax.ShapeDtypeStruct((SRC, 128), F32),
        ),
        scratch_shapes=[
            pltpu.VMEM((16, N_WIN * 128), BF16),
            pltpu.VMEM((128, N_WIN * 128), BF16),
        ],
        compiler_params=pltpu.CompilerParams(vmem_limit_bytes=8 << 20),
        name="window",
    )(vals, ray, q, beta)


def end_kernel(norm_ref, q_ref, *refs):
    mine, theirs = refs[0:ITERS], refs[ITERS : 2 * ITERS]
    alphas = [r[...] for r in refs[2 * ITERS : 3 * ITERS]]
    betas = [r[...] for r in refs[3 * ITERS : 4 * ITERS]]
    update_ref, data_ref = refs[4 * ITERS :]
    betas.append(jnp.sqrt(jnp.sum(norm_ref[...], axis=0, keepdims=True)))
    data_ref[...] = q_ref[...] / jnp.broadcast_to(betas[ITERS], (RT, 128))
    one = jnp.ones_like(alphas[0])
    phibar, rhobar = betas[0], alphas[0]
    search = [one]
    update = [jnp.zeros_like(one) for _ in range(ITERS)]
    for step in range(ITERS):
        beta = betas[step + 1]
        rho = jnp.sqrt(rhobar * rhobar + beta * beta)
        cosine = rhobar / rho
        sine = beta / rho
        phi = cosine * phibar
        phibar = sine * phibar
        for i, s in enumerate(search):
            update[i] = update[i] + phi / rho * s
        if step + 1 < ITERS:
            theta = sine * alphas[step + 1]
            rhobar = -cosine * alphas[step + 1]
            search = [-(theta / rho * s) for s in search] + [one]
    scale = [jnp.broadcast_to(u / a, (CC, 128)) for u, a in zip(update, alphas)]
    core = lax.axis_index("off")
    for refs_in, half in ((mine, core), (theirs, 1 - core)):
        at = pl.ds(pl.multiple_of(half * CC, CC), CC)
        for t in range(BLK_DEV // 128):
            cols = slice(t * 128, (t + 1) * 128)
            total = refs_in[0][:, cols] * scale[0]
            for i in range(1, ITERS):
                total = total + refs_in[i][:, cols] * scale[i]
            update_ref[at, cols] = total


def end_call(norm, q, mine, theirs, alphas, betas):
    return pl.pallas_call(
        end_kernel,
        out_shape=(
            jax.ShapeDtypeStruct((CELLS, BLK_DEV), F32),
            jax.ShapeDtypeStruct((RT, 128), F32),
        ),
        compiler_params=pltpu.CompilerParams(vmem_limit_bytes=8 << 20),
        name="end",
    )(norm, q, *mine, *theirs, *alphas, *betas)


def exchange(x):
    rest = x.shape[0] // SRC
    y = lax.all_to_all(x.reshape(SRC, rest, 128), ("win", "off"), 0, 0, tiled=True)
    return y.reshape(x.shape)


def body(kernels, blocks, counts, ray_of, slopes):
    ray = ray_of.reshape(N_WIN, CAP)
    q = slopes.reshape(RT, 128)
    k = start_call(
        kernels.reshape(SRC, CC, CAP), blocks.reshape(N_WIN, CAP), counts.reshape(1, N_WIN), ray, q
    )
    k = lax.all_to_all(k, ("win", "off"), 0, 0, tiled=True)
    mine, theirs, alphas, betas = [], [], [], []
    for step in range(ITERS):
        if step == 0:
            prev, vals, beta, ids, oh = owner_call(True, k)
        else:
            prev, vals, beta = owner_call(False, k, oh, ids, weights, prev, alpha)
        mine.append(prev)
        theirs.append(lax.ppermute(prev, "off", [(0, 1), (1, 0)]))
        betas.append(beta)
        weights, q, alpha, norm = window_call(exchange(vals), ray, q, beta)
        alphas.append(alpha)
        weights = exchange(weights)
    owner_call(False, k, oh, ids, weights, prev, alpha)
    update, data = end_call(exchange(norm), q, mine, theirs, alphas, betas)
    return update, data.reshape(1, 1, RAYS)


def solution(mesh):
    in_specs = (
        P("off", "win", None, None, None),
        P("off", "win", None, None),
        P("off", "win", None),
        P("off", "win", None, None),
        P("off", "win", None),
    )
    out_specs = (P(None, "win"), P("off", "win", None))
    return jax.shard_map(body, mesh=mesh, in_specs=in_specs, out_specs=out_specs, check_vma=False)
```

```python
import functools

import jax
import jax.numpy as jnp
from jax import lax
from jax.experimental import pallas as pl
from jax.experimental.pallas import tpu as pltpu
from jax.sharding import PartitionSpec as P

CELLS = 64
CAP = 128
BLK_DEV = 2048
RAYS = 512
ITERS = 3
N_OFF = 2
N_WIN = 64
SRC = N_OFF * N_WIN
CC = CELLS // N_OFF
RT = RAYS // 128
HI = 8
LO = BLK_DEV // HI
CA = 16
CF = 8
SLAB = CC + 8
F32 = jnp.float32
BF16 = jnp.bfloat16


def rows(ref, start, count, stride):
    return ref[pl.ds(start, count, stride=stride), :]


def gather_rays(data, ray, out_ref, first, half, whole):
    lo = jnp.bitwise_and(ray, 127)
    hi = jnp.right_shift(ray, 7)
    parts = []
    for g in range(N_WIN // 8):
        lo_g, hi_g = lo[g * 8 : g * 8 + 8], hi[g * 8 : g * 8 + 8]
        acc = jnp.zeros((8, 128), F32)
        for t in range(RT):
            table = jnp.broadcast_to(data[t : t + 1], (8, 128))
            got = jnp.take_along_axis(table, lo_g, axis=1, mode="promise_in_bounds")
            acc = jnp.where(hi_g == t, got, acc)
        parts.append(acc)
    weights = jnp.concatenate(parts, axis=0)
    out_ref[pl.ds(first, N_WIN, stride=whole), :] = weights
    out_ref[pl.ds(first + half, N_WIN, stride=whole), :] = weights


def start_kernel(k_ref, blocks_in, counts_in, ray_in, slopes_in, out_ref, *scratch):
    blocks_ref, counts_ref, ray_ref, slopes_ref, extra_ref, sems = scratch
    rows_out = pltpu.make_async_copy(k_ref, out_ref.at[:, 0:CC, :], sems.at[0])
    rows_out.start()
    loads = [
        pltpu.make_async_copy(src, dst, sems.at[2 + n])
        for n, (src, dst) in enumerate(
            ((blocks_in, blocks_ref), (counts_in, counts_ref), (ray_in, ray_ref), (slopes_in, slopes_ref))
        )
    ]
    for load in loads:
        load.start()
    for load in loads:
        load.wait()
    slot = lax.broadcasted_iota(jnp.int32, (N_WIN, CAP), 1)
    row = lax.broadcasted_iota(jnp.int32, (N_WIN, N_WIN), 0)
    col = lax.broadcasted_iota(jnp.int32, (N_WIN, N_WIN), 1)
    counts = jnp.broadcast_to(counts_ref[...].astype(F32), (N_WIN, N_WIN))
    counts = jnp.sum(jnp.where(row == col, counts, 0.0), axis=1, keepdims=True)
    ids = jnp.where(slot.astype(F32) < counts, blocks_ref[...].astype(F32), -1.0)
    extra_ref[...] = jnp.zeros_like(extra_ref)
    extra_ref[pl.ds(0, N_WIN, stride=16), :] = ids
    extra_ref[pl.ds(8, N_WIN, stride=16), :] = ids
    data = slopes_ref[...]
    gather_rays(data, ray_ref[...], extra_ref, 1, 8, 16)
    extra_ref[pl.ds(2, SRC, stride=8), :] = jnp.full((SRC, 128), jnp.sum(data * data), F32)
    extra_out = pltpu.make_async_copy(
        extra_ref.reshape(SRC, 8, 128), out_ref.at[:, CC:SLAB, :], sems.at[1]
    )
    extra_out.start()
    rows_out.wait()
    extra_out.wait()


def start_call(k, blocks, counts, ray, slopes):
    return pl.pallas_call(
        start_kernel,
        out_shape=jax.ShapeDtypeStruct((SRC, SLAB, 128), F32),
        in_specs=[pl.BlockSpec(memory_space=pltpu.HBM)] * 5,
        out_specs=pl.BlockSpec(memory_space=pltpu.HBM),
        scratch_shapes=[
            pltpu.VMEM((N_WIN, CAP), jnp.int32),
            pltpu.VMEM((1, N_WIN), jnp.int32),
            pltpu.VMEM((N_WIN, CAP), jnp.int32),
            pltpu.VMEM((RT, 128), F32),
            pltpu.VMEM((8 * SRC, 128), F32),
            pltpu.SemaphoreType.DMA((6,)),
        ],
        compiler_params=pltpu.CompilerParams(vmem_limit_bytes=4 << 20),
        name="start",
    )(*(pltpu.with_memory_space_constraint(x, pltpu.HBM) for x in (k, blocks, counts, ray, slopes)))


def owner_kernel(first, k_ref, *refs):
    if first:
        p_ref, vals_ref, beta_ref, ids_ref, *scratch = refs
        ids_ref[...] = k_ref[:, CC, :].astype(jnp.int32)
        norms = k_ref[:, CC + 2, :]
        weight_of = lambda s: k_ref[s, CC + 1 : CC + 2, :]
    else:
        ids_ref, wts_ref, pprev_ref, aprev_ref, p_ref, vals_ref, beta_ref, *scratch = refs
        norms = rows(wts_ref, 1, SRC, 2)
        weight_of = lambda s: wts_ref[pl.ds(2 * s, 1), :]
    oh_ref, y0_ref, y1_ref, acc_ref, v_ref, g0_ref, g1_ref = scratch
    steps = SRC // CA
    beta = jnp.sqrt(jnp.sum(norms, axis=0, keepdims=True))
    beta_ref[...] = beta
    acc_ref[...] = jnp.zeros_like(acc_ref)
    lo_iota = lax.broadcasted_iota(jnp.int32, (LO, 128), 0).astype(F32).astype(BF16)

    def spread(y_ref, i):
        for c in range(CA):
            s = i * CA + c
            at = slice(c * 128, (c + 1) * 128)
            blk = ids_ref[pl.ds(s, 1), :]
            hi = jnp.right_shift(blk, 8)
            lo = jnp.where(blk < 0, -1, jnp.bitwise_and(blk, LO - 1)).astype(F32)
            hit = lo_iota == jnp.broadcast_to(lo, (LO, 128)).astype(BF16)
            oh_ref[:, pl.ds(pl.multiple_of(s * 128, 128), 128)] = jnp.where(
                hit, jnp.ones((LO, 128), BF16), jnp.zeros((LO, 128), BF16)
            )
            x = k_ref[s, 0:CC, :] * jnp.broadcast_to(weight_of(s), (CC, 128))
            x1 = x.astype(BF16)
            x2 = (x - x1.astype(F32)).astype(BF16)
            hib = jnp.broadcast_to(hi.astype(F32), (CC, 128)).astype(BF16)
            zero = jnp.zeros((CC, 128), BF16)
            for h in range(HI):
                m = hib == jnp.asarray(h, BF16)
                y_ref[2 * h * CC : (2 * h + 1) * CC, at] = jnp.where(m, x1, zero)
                y_ref[(2 * h + 1) * CC : (2 * h + 2) * CC, at] = jnp.where(m, x2, zero)

    def add(y_ref, i):
        oh = oh_ref[:, pl.ds(pl.multiple_of(i * CA * 128, CA * 128), CA * 128)]
        acc_ref[...] += lax.dot_general(
            y_ref[...], oh, (((1,), (1,)), ((), ())), preferred_element_type=F32
        )

    def add_two(t, carry):
        add(y0_ref, 2 * t)
        spread(y1_ref, 2 * t + 1)
        add(y1_ref, 2 * t + 1)
        spread(y0_ref, 2 * t + 2)
        return carry

    steps = SRC // CA
    spread(y0_ref, 0)
    lax.fori_loop(0, steps // 2 - 1, add_two, 0)
    add(y0_ref, steps - 2)
    spread(y1_ref, steps - 1)
    add(y1_ref, steps - 1)

    squares = jnp.zeros((8, 128), F32)
    beta_b = jnp.broadcast_to(beta, (CC, 128))
    if not first:
        back = jnp.broadcast_to(beta / aprev_ref[...], (CC, 128))
    for h in range(HI):
        for t in range(LO // 128):
            at = slice(t * 128, (t + 1) * 128)
            g = acc_ref[2 * h * CC : (2 * h + 1) * CC, at] + acc_ref[(2 * h + 1) * CC : (2 * h + 2) * CC, at]
            g = g / beta_b
            cols = slice(h * LO + t * 128, h * LO + (t + 1) * 128)
            if not first:
                g = g - pprev_ref[:, cols] * back
            p_ref[:, cols] = g
            g1 = g.astype(BF16)
            v_ref[h * CC : (h + 1) * CC, at] = g1
            v_ref[(HI + h) * CC : (HI + h + 1) * CC, at] = (g - g1.astype(F32)).astype(BF16)
            g2 = g * g
            squares = squares + g2[0:8] + g2[8:16] + g2[16:24] + g2[24:32]
    vals_ref[pl.ds(1, SRC, stride=2), :] = jnp.full((SRC, 128), jnp.sum(squares), F32)

    def fetch(g_ref, i):
        oh = oh_ref[:, pl.ds(pl.multiple_of(i * CF * 128, CF * 128), CF * 128)]
        g_ref[...] = lax.dot_general(v_ref[...], oh, (((1,), (0,)), ((), ())), preferred_element_type=F32)

    def use(g_ref, i):
        for c in range(CF):
            s = i * CF + c
            at = slice(c * 128, (c + 1) * 128)
            hi = jnp.broadcast_to(jnp.right_shift(ids_ref[pl.ds(s, 1), :], 8), (8, 128))
            ks = [k_ref[s, j : j + 8, :] for j in range(0, CC, 8)]
            total = jnp.zeros((8, 128), F32)
            for h in range(HI):
                part = None
                for j, kj in zip(range(0, CC, 8), ks):
                    r = h * CC + j
                    e = (g_ref[r : r + 8, at] + g_ref[HI * CC + r : HI * CC + r + 8, at]) * kj
                    part = e if part is None else part + e
                total = jnp.where(hi == h, part, total)
            vals_ref[pl.ds(2 * s, 1), :] = jnp.sum(total, axis=0, keepdims=True)

    def fetch_two(t, carry):
        fetch(g1_ref, 2 * t + 1)
        use(g0_ref, 2 * t)
        fetch(g0_ref, 2 * t + 2)
        use(g1_ref, 2 * t + 1)
        return carry

    last = SRC // CF - 1
    fetch(g0_ref, 0)
    lax.fori_loop(0, last // 2, fetch_two, 0)
    fetch(g1_ref, last)
    use(g0_ref, last - 1)
    use(g1_ref, last)


def owner_call(first, *args):
    outs = [
        jax.ShapeDtypeStruct((CC, BLK_DEV), F32),
        jax.ShapeDtypeStruct((2 * SRC, 128), F32),
        jax.ShapeDtypeStruct((1, 128), F32),
    ]
    if first:
        outs.append(jax.ShapeDtypeStruct((SRC, 128), jnp.int32))
    return pl.pallas_call(
        functools.partial(owner_kernel, first),
        out_shape=tuple(outs),
        scratch_shapes=[
            pltpu.VMEM((LO, SRC * 128), BF16),
            pltpu.VMEM((2 * HI * CC, CA * 128), BF16),
            pltpu.VMEM((2 * HI * CC, CA * 128), BF16),
            pltpu.VMEM((2 * HI * CC, LO), F32),
            pltpu.VMEM((2 * HI * CC, LO), BF16),
            pltpu.VMEM((2 * HI * CC, CF * 128), F32),
            pltpu.VMEM((2 * HI * CC, CF * 128), F32),
        ],
        compiler_params=pltpu.CompilerParams(vmem_limit_bytes=32 << 20),
        name="owner",
    )(*args)


def window_kernel(vals_ref, ray_ref, q_ref, beta_ref, wts_ref, qout_ref, alpha_ref, norm_ref, a_ref, b_ref):
    alpha = jnp.sqrt(jnp.sum(rows(vals_ref, 1, SRC, 2), axis=0, keepdims=True))
    alpha_ref[...] = alpha
    vals = rows(vals_ref, 0, N_WIN, 4) + rows(vals_ref, 2, N_WIN, 4)
    v1 = vals.astype(BF16).astype(F32)
    v2 = (vals - v1).astype(BF16).astype(F32)
    v3 = vals - v1 - v2
    ray = ray_ref[...]
    lo = jnp.bitwise_and(ray, 127)
    hi = jnp.right_shift(ray, 7)
    sub = lax.broadcasted_iota(jnp.int32, (8, 128), 0)
    tier = jnp.bitwise_and(sub, RT - 1)
    lo_iota = lax.broadcasted_iota(jnp.int32, (128, 128), 0)
    wide = lambda r, p, n: jnp.broadcast_to(r[p : p + 1], (n, 128))
    for p in range(N_WIN):
        at = slice(p * 128, (p + 1) * 128)
        hit = tier == wide(hi, p, 8)
        upper = jnp.where(sub < RT, wide(v1, p, 8), wide(v2, p, 8))
        lower = jnp.where(sub < RT, wide(v3, p, 8), 0.0)
        both = jnp.concatenate([jnp.where(hit, upper, 0.0), jnp.where(hit, lower, 0.0)], axis=0)
        a_ref[:, at] = both.astype(BF16)
        b_ref[:, at] = jnp.where(lo_iota == wide(lo, p, 128), 1.0, 0.0).astype(BF16)
    out = lax.dot_general(a_ref[...], b_ref[...], (((1,), (1,)), ((), ())), preferred_element_type=F32)
    summed = out[0:RT] + out[RT : 2 * RT] + out[2 * RT : 3 * RT]
    alpha_b = jnp.broadcast_to(alpha, (RT, 128))
    beta_b = jnp.broadcast_to(beta_ref[...], (RT, 128))
    q = summed / alpha_b - alpha_b * (q_ref[...] / beta_b)
    qout_ref[...] = q
    part = jnp.sum(q * q)
    gather_rays(q, ray, wts_ref, 0, 2, 4)
    wts_ref[pl.ds(1, SRC, stride=2), :] = jnp.full((SRC, 128), part, F32)
    norm_ref[...] = jnp.full((SRC, 128), part, F32)


def window_call(vals, ray, q, beta):
    return pl.pallas_call(
        window_kernel,
        out_shape=(
            jax.ShapeDtypeStruct((2 * SRC, 128), F32),
            jax.ShapeDtypeStruct((RT, 128), F32),
            jax.ShapeDtypeStruct((1, 128), F32),
            jax.ShapeDtypeStruct((SRC, 128), F32),
        ),
        scratch_shapes=[
            pltpu.VMEM((16, N_WIN * 128), BF16),
            pltpu.VMEM((128, N_WIN * 128), BF16),
        ],
        compiler_params=pltpu.CompilerParams(vmem_limit_bytes=8 << 20),
        name="window",
    )(vals, ray, q, beta)


def end_kernel(norm_ref, q_ref, *refs):
    mine, theirs = refs[0:ITERS], refs[ITERS : 2 * ITERS]
    alphas = [r[...] for r in refs[2 * ITERS : 3 * ITERS]]
    betas = [r[...] for r in refs[3 * ITERS : 4 * ITERS]]
    update_ref, data_ref = refs[4 * ITERS :]
    betas.append(jnp.sqrt(jnp.sum(norm_ref[...], axis=0, keepdims=True)))
    data_ref[...] = q_ref[...] / jnp.broadcast_to(betas[ITERS], (RT, 128))
    one = jnp.ones_like(alphas[0])
    phibar, rhobar = betas[0], alphas[0]
    search = [one]
    update = [jnp.zeros_like(one) for _ in range(ITERS)]
    for step in range(ITERS):
        beta = betas[step + 1]
        rho = jnp.sqrt(rhobar * rhobar + beta * beta)
        cosine = rhobar / rho
        sine = beta / rho
        phi = cosine * phibar
        phibar = sine * phibar
        for i, s in enumerate(search):
            update[i] = update[i] + phi / rho * s
        if step + 1 < ITERS:
            theta = sine * alphas[step + 1]
            rhobar = -cosine * alphas[step + 1]
            search = [-(theta / rho * s) for s in search] + [one]
    scale = [jnp.broadcast_to(u / a, (CC, 128)) for u, a in zip(update, alphas)]
    core = lax.axis_index("off")
    for refs_in, half in ((mine, core), (theirs, 1 - core)):
        at = pl.ds(pl.multiple_of(half * CC, CC), CC)
        for t in range(BLK_DEV // 128):
            cols = slice(t * 128, (t + 1) * 128)
            total = refs_in[0][:, cols] * scale[0]
            for i in range(1, ITERS):
                total = total + refs_in[i][:, cols] * scale[i]
            update_ref[at, cols] = total


def end_call(norm, q, mine, theirs, alphas, betas):
    return pl.pallas_call(
        end_kernel,
        out_shape=(
            jax.ShapeDtypeStruct((CELLS, BLK_DEV), F32),
            jax.ShapeDtypeStruct((RT, 128), F32),
        ),
        compiler_params=pltpu.CompilerParams(vmem_limit_bytes=8 << 20),
        name="end",
    )(norm, q, *mine, *theirs, *alphas, *betas)


def exchange(x):
    rest = x.shape[0] // SRC
    y = lax.all_to_all(x.reshape(SRC, rest, 128), ("win", "off"), 0, 0, tiled=True)
    return y.reshape(x.shape)


def body(kernels, blocks, counts, ray_of, slopes):
    ray = ray_of.reshape(N_WIN, CAP)
    q = slopes.reshape(RT, 128)
    k = start_call(
        kernels.reshape(SRC, CC, CAP), blocks.reshape(N_WIN, CAP), counts.reshape(1, N_WIN), ray, q
    )
    k = lax.all_to_all(k, ("win", "off"), 0, 0, tiled=True)
    mine, theirs, alphas, betas = [], [], [], []
    for step in range(ITERS):
        if step == 0:
            prev, vals, beta, ids = owner_call(True, k)
        else:
            prev, vals, beta = owner_call(False, k, ids, weights, prev, alpha)
        mine.append(prev)
        theirs.append(lax.ppermute(prev, "off", [(0, 1), (1, 0)]))
        betas.append(beta)
        weights, q, alpha, norm = window_call(exchange(vals), ray, q, beta)
        alphas.append(alpha)
        weights = exchange(weights)
    owner_call(False, k, ids, weights, prev, alpha)
    update, data = end_call(exchange(norm), q, mine, theirs, alphas, betas)
    return update, data.reshape(1, 1, RAYS)


def solution(mesh):
    in_specs = (
        P("off", "win", None, None, None),
        P("off", "win", None, None),
        P("off", "win", None),
        P("off", "win", None, None),
        P("off", "win", None),
    )
    out_specs = (P(None, "win"), P("off", "win", None))
    return jax.shard_map(body, mesh=mesh, in_specs=in_specs, out_specs=out_specs, check_vma=False)
```

```python
import functools

import jax
import jax.numpy as jnp
from jax import lax
from jax.experimental import pallas as pl
from jax.experimental.pallas import tpu as pltpu
from jax.sharding import PartitionSpec as P

CELLS = 64
CAP = 128
BLK_DEV = 2048
RAYS = 512
ITERS = 3
N_OFF = 2
N_WIN = 64
SRC = N_OFF * N_WIN
CC = CELLS // N_OFF
RT = RAYS // 128
HI = 8
LO = BLK_DEV // HI
CA = 16
CF = 8
SLAB = CC + 8
F32 = jnp.float32
BF16 = jnp.bfloat16


def rows(ref, start, count, stride):
    return ref[pl.ds(start, count, stride=stride), :]


def gather_rays(data, ray, out_ref, first, half, whole):
    lo = jnp.bitwise_and(ray, 127)
    hi = jnp.right_shift(ray, 7)
    parts = []
    for g in range(N_WIN // 8):
        lo_g, hi_g = lo[g * 8 : g * 8 + 8], hi[g * 8 : g * 8 + 8]
        acc = jnp.zeros((8, 128), F32)
        for t in range(RT):
            table = jnp.broadcast_to(data[t : t + 1], (8, 128))
            got = jnp.take_along_axis(table, lo_g, axis=1, mode="promise_in_bounds")
            acc = jnp.where(hi_g == t, got, acc)
        parts.append(acc)
    weights = jnp.concatenate(parts, axis=0)
    out_ref[pl.ds(first, N_WIN, stride=whole), :] = weights
    out_ref[pl.ds(first + half, N_WIN, stride=whole), :] = weights


def start_kernel(k_ref, blocks_in, counts_in, ray_in, slopes_in, out_ref, *scratch):
    blocks_ref, counts_ref, ray_ref, slopes_ref, extra_ref, sems = scratch
    rows_out = pltpu.make_async_copy(k_ref, out_ref.at[:, 0:CC, :], sems.at[0])
    rows_out.start()
    loads = [
        pltpu.make_async_copy(src, dst, sems.at[2 + n])
        for n, (src, dst) in enumerate(
            ((blocks_in, blocks_ref), (counts_in, counts_ref), (ray_in, ray_ref), (slopes_in, slopes_ref))
        )
    ]
    for load in loads:
        load.start()
    for load in loads:
        load.wait()
    slot = lax.broadcasted_iota(jnp.int32, (N_WIN, CAP), 1)
    row = lax.broadcasted_iota(jnp.int32, (N_WIN, N_WIN), 0)
    col = lax.broadcasted_iota(jnp.int32, (N_WIN, N_WIN), 1)
    counts = jnp.broadcast_to(counts_ref[...].astype(F32), (N_WIN, N_WIN))
    counts = jnp.sum(jnp.where(row == col, counts, 0.0), axis=1, keepdims=True)
    ids = jnp.where(slot.astype(F32) < counts, blocks_ref[...].astype(F32), -1.0)
    extra_ref[...] = jnp.zeros_like(extra_ref)
    extra_ref[pl.ds(0, N_WIN, stride=16), :] = ids
    extra_ref[pl.ds(8, N_WIN, stride=16), :] = ids
    data = slopes_ref[...]
    gather_rays(data, ray_ref[...], extra_ref, 1, 8, 16)
    extra_ref[pl.ds(2, SRC, stride=8), :] = jnp.full((SRC, 128), jnp.sum(data * data), F32)
    extra_out = pltpu.make_async_copy(
        extra_ref.reshape(SRC, 8, 128), out_ref.at[:, CC:SLAB, :], sems.at[1]
    )
    extra_out.start()
    rows_out.wait()
    extra_out.wait()


def start_call(k, blocks, counts, ray, slopes):
    return pl.pallas_call(
        start_kernel,
        out_shape=pltpu.HBM((SRC, SLAB, 128), F32),
        in_specs=[pl.BlockSpec(memory_space=pltpu.HBM)] * 5,
        out_specs=pl.BlockSpec(memory_space=pltpu.HBM),
        scratch_shapes=[
            pltpu.VMEM((N_WIN, CAP), jnp.int32),
            pltpu.VMEM((1, N_WIN), jnp.int32),
            pltpu.VMEM((N_WIN, CAP), jnp.int32),
            pltpu.VMEM((RT, 128), F32),
            pltpu.VMEM((8 * SRC, 128), F32),
            pltpu.SemaphoreType.DMA((6,)),
        ],
        compiler_params=pltpu.CompilerParams(vmem_limit_bytes=4 << 20),
        name="start",
    )(*(pltpu.with_memory_space_constraint(x, pltpu.HBM) for x in (k, blocks, counts, ray, slopes)))


def owner_kernel(first, k_ref, *refs):
    if first:
        p_ref, vals_ref, beta_ref, ids_ref, oh_hbm, oh_ref, sem, *scratch = refs
        ids_ref[...] = k_ref[:, CC, :].astype(jnp.int32)
        norms = k_ref[:, CC + 2, :]
        weight_of = lambda s: k_ref[s, CC + 1 : CC + 2, :]
    else:
        oh_ref, ids_ref, wts_ref, pprev_ref, aprev_ref, p_ref, vals_ref, beta_ref, *scratch = refs
        norms = rows(wts_ref, 1, SRC, 2)
        weight_of = lambda s: wts_ref[pl.ds(2 * s, 1), :]
    y0_ref, y1_ref, acc_ref, v_ref, g0_ref, g1_ref = scratch
    steps = SRC // CA
    beta = jnp.sqrt(jnp.sum(norms, axis=0, keepdims=True))
    beta_ref[...] = beta
    acc_ref[...] = jnp.zeros_like(acc_ref)
    lo_iota = lax.broadcasted_iota(jnp.int32, (LO, 128), 0).astype(F32).astype(BF16)

    def spread(y_ref, i):
        for c in range(CA):
            s = i * CA + c
            at = slice(c * 128, (c + 1) * 128)
            blk = ids_ref[pl.ds(s, 1), :]
            hi = jnp.right_shift(blk, 8)
            if first:
                lo = jnp.where(blk < 0, -1, jnp.bitwise_and(blk, LO - 1)).astype(F32)
                hit = lo_iota == jnp.broadcast_to(lo, (LO, 128)).astype(BF16)
                oh_ref[:, pl.ds(pl.multiple_of(s * 128, 128), 128)] = jnp.where(
                    hit, jnp.ones((LO, 128), BF16), jnp.zeros((LO, 128), BF16)
                )
            x = k_ref[s, 0:CC, :] * jnp.broadcast_to(weight_of(s), (CC, 128))
            x1 = x.astype(BF16)
            x2 = (x - x1.astype(F32)).astype(BF16)
            hib = jnp.broadcast_to(hi.astype(F32), (CC, 128)).astype(BF16)
            zero = jnp.zeros((CC, 128), BF16)
            for h in range(HI):
                m = hib == jnp.asarray(h, BF16)
                y_ref[2 * h * CC : (2 * h + 1) * CC, at] = jnp.where(m, x1, zero)
                y_ref[(2 * h + 1) * CC : (2 * h + 2) * CC, at] = jnp.where(m, x2, zero)

    def add(y_ref, i):
        oh = oh_ref[:, pl.ds(pl.multiple_of(i * CA * 128, CA * 128), CA * 128)]
        acc_ref[...] += lax.dot_general(
            y_ref[...], oh, (((1,), (1,)), ((), ())), preferred_element_type=F32
        )

    def add_two(t, carry):
        add(y0_ref, 2 * t)
        spread(y1_ref, 2 * t + 1)
        add(y1_ref, 2 * t + 1)
        spread(y0_ref, 2 * t + 2)
        return carry

    steps = SRC // CA
    spread(y0_ref, 0)
    lax.fori_loop(0, steps // 2 - 1, add_two, 0)
    add(y0_ref, steps - 2)
    spread(y1_ref, steps - 1)
    add(y1_ref, steps - 1)

    if first:
        keep = pltpu.make_async_copy(oh_ref, oh_hbm, sem)
        keep.start()
    squares = jnp.zeros((8, 128), F32)
    beta_b = jnp.broadcast_to(beta, (CC, 128))
    if not first:
        back = jnp.broadcast_to(beta / aprev_ref[...], (CC, 128))
    for h in range(HI):
        for t in range(LO // 128):
            at = slice(t * 128, (t + 1) * 128)
            g = acc_ref[2 * h * CC : (2 * h + 1) * CC, at] + acc_ref[(2 * h + 1) * CC : (2 * h + 2) * CC, at]
            g = g / beta_b
            cols = slice(h * LO + t * 128, h * LO + (t + 1) * 128)
            if not first:
                g = g - pprev_ref[:, cols] * back
            p_ref[:, cols] = g
            g1 = g.astype(BF16)
            v_ref[h * CC : (h + 1) * CC, at] = g1
            v_ref[(HI + h) * CC : (HI + h + 1) * CC, at] = (g - g1.astype(F32)).astype(BF16)
            g2 = g * g
            squares = squares + g2[0:8] + g2[8:16] + g2[16:24] + g2[24:32]
    vals_ref[pl.ds(1, SRC, stride=2), :] = jnp.full((SRC, 128), jnp.sum(squares), F32)

    def fetch(g_ref, i):
        oh = oh_ref[:, pl.ds(pl.multiple_of(i * CF * 128, CF * 128), CF * 128)]
        g_ref[...] = lax.dot_general(v_ref[...], oh, (((1,), (0,)), ((), ())), preferred_element_type=F32)

    def use(g_ref, i):
        for c in range(CF):
            s = i * CF + c
            at = slice(c * 128, (c + 1) * 128)
            hi = jnp.broadcast_to(jnp.right_shift(ids_ref[pl.ds(s, 1), :], 8), (8, 128))
            ks = [k_ref[s, j : j + 8, :] for j in range(0, CC, 8)]
            total = jnp.zeros((8, 128), F32)
            for h in range(HI):
                part = None
                for j, kj in zip(range(0, CC, 8), ks):
                    r = h * CC + j
                    e = (g_ref[r : r + 8, at] + g_ref[HI * CC + r : HI * CC + r + 8, at]) * kj
                    part = e if part is None else part + e
                total = jnp.where(hi == h, part, total)
            vals_ref[pl.ds(2 * s, 1), :] = jnp.sum(total, axis=0, keepdims=True)

    def fetch_two(t, carry):
        fetch(g1_ref, 2 * t + 1)
        use(g0_ref, 2 * t)
        fetch(g0_ref, 2 * t + 2)
        use(g1_ref, 2 * t + 1)
        return carry

    last = SRC // CF - 1
    fetch(g0_ref, 0)
    lax.fori_loop(0, last // 2, fetch_two, 0)
    fetch(g1_ref, last)
    use(g0_ref, last - 1)
    use(g1_ref, last)
    if first:
        keep.wait()


def owner_call(first, *args):
    outs = [
        jax.ShapeDtypeStruct((CC, BLK_DEV), F32),
        jax.ShapeDtypeStruct((2 * SRC, 128), F32),
        jax.ShapeDtypeStruct((1, 128), F32),
    ]
    out_specs = [pl.BlockSpec(memory_space=pltpu.VMEM)] * len(outs)
    scratch = []
    if first:
        outs.append(jax.ShapeDtypeStruct((SRC, 128), jnp.int32))
        outs.append(pltpu.HBM((LO, SRC * 128), BF16))
        out_specs.append(pl.BlockSpec(memory_space=pltpu.VMEM))
        out_specs.append(pl.BlockSpec(memory_space=pltpu.HBM))
        scratch = [pltpu.VMEM((LO, SRC * 128), BF16), pltpu.SemaphoreType.DMA]
    return pl.pallas_call(
        functools.partial(owner_kernel, first),
        out_shape=tuple(outs),
        out_specs=tuple(out_specs),
        scratch_shapes=scratch
        + [
            pltpu.VMEM((2 * HI * CC, CA * 128), BF16),
            pltpu.VMEM((2 * HI * CC, CA * 128), BF16),
            pltpu.VMEM((2 * HI * CC, LO), F32),
            pltpu.VMEM((2 * HI * CC, LO), BF16),
            pltpu.VMEM((2 * HI * CC, CF * 128), F32),
            pltpu.VMEM((2 * HI * CC, CF * 128), F32),
        ],
        compiler_params=pltpu.CompilerParams(vmem_limit_bytes=(30 if first else 20) << 20),
        name="owner",
    )(*args)


def window_kernel(vals_ref, ray_ref, q_ref, beta_ref, wts_ref, qout_ref, alpha_ref, norm_ref, a_ref, b_ref):
    alpha = jnp.sqrt(jnp.sum(rows(vals_ref, 1, SRC, 2), axis=0, keepdims=True))
    alpha_ref[...] = alpha
    vals = rows(vals_ref, 0, N_WIN, 4) + rows(vals_ref, 2, N_WIN, 4)
    v1 = vals.astype(BF16).astype(F32)
    v2 = (vals - v1).astype(BF16).astype(F32)
    v3 = vals - v1 - v2
    ray = ray_ref[...]
    lo = jnp.bitwise_and(ray, 127)
    hi = jnp.right_shift(ray, 7)
    sub = lax.broadcasted_iota(jnp.int32, (8, 128), 0)
    tier = jnp.bitwise_and(sub, RT - 1)
    lo_iota = lax.broadcasted_iota(jnp.int32, (128, 128), 0)
    wide = lambda r, p, n: jnp.broadcast_to(r[p : p + 1], (n, 128))
    for p in range(N_WIN):
        at = slice(p * 128, (p + 1) * 128)
        hit = tier == wide(hi, p, 8)
        upper = jnp.where(sub < RT, wide(v1, p, 8), wide(v2, p, 8))
        lower = jnp.where(sub < RT, wide(v3, p, 8), 0.0)
        both = jnp.concatenate([jnp.where(hit, upper, 0.0), jnp.where(hit, lower, 0.0)], axis=0)
        a_ref[:, at] = both.astype(BF16)
        b_ref[:, at] = jnp.where(lo_iota == wide(lo, p, 128), 1.0, 0.0).astype(BF16)
    out = lax.dot_general(a_ref[...], b_ref[...], (((1,), (1,)), ((), ())), preferred_element_type=F32)
    summed = out[0:RT] + out[RT : 2 * RT] + out[2 * RT : 3 * RT]
    alpha_b = jnp.broadcast_to(alpha, (RT, 128))
    beta_b = jnp.broadcast_to(beta_ref[...], (RT, 128))
    q = summed / alpha_b - alpha_b * (q_ref[...] / beta_b)
    qout_ref[...] = q
    part = jnp.sum(q * q)
    gather_rays(q, ray, wts_ref, 0, 2, 4)
    wts_ref[pl.ds(1, SRC, stride=2), :] = jnp.full((SRC, 128), part, F32)
    norm_ref[...] = jnp.full((SRC, 128), part, F32)


def window_call(vals, ray, q, beta):
    return pl.pallas_call(
        window_kernel,
        out_shape=(
            jax.ShapeDtypeStruct((2 * SRC, 128), F32),
            jax.ShapeDtypeStruct((RT, 128), F32),
            jax.ShapeDtypeStruct((1, 128), F32),
            jax.ShapeDtypeStruct((SRC, 128), F32),
        ),
        scratch_shapes=[
            pltpu.VMEM((16, N_WIN * 128), BF16),
            pltpu.VMEM((128, N_WIN * 128), BF16),
        ],
        compiler_params=pltpu.CompilerParams(vmem_limit_bytes=8 << 20),
        name="window",
    )(vals, ray, q, beta)


def end_kernel(norm_ref, q_ref, *refs):
    mine, theirs = refs[0:ITERS], refs[ITERS : 2 * ITERS]
    alphas = [r[...] for r in refs[2 * ITERS : 3 * ITERS]]
    betas = [r[...] for r in refs[3 * ITERS : 4 * ITERS]]
    update_ref, data_ref = refs[4 * ITERS :]
    betas.append(jnp.sqrt(jnp.sum(norm_ref[...], axis=0, keepdims=True)))
    data_ref[...] = q_ref[...] / jnp.broadcast_to(betas[ITERS], (RT, 128))
    one = jnp.ones_like(alphas[0])
    phibar, rhobar = betas[0], alphas[0]
    search = [one]
    update = [jnp.zeros_like(one) for _ in range(ITERS)]
    for step in range(ITERS):
        beta = betas[step + 1]
        rho = jnp.sqrt(rhobar * rhobar + beta * beta)
        cosine = rhobar / rho
        sine = beta / rho
        phi = cosine * phibar
        phibar = sine * phibar
        for i, s in enumerate(search):
            update[i] = update[i] + phi / rho * s
        if step + 1 < ITERS:
            theta = sine * alphas[step + 1]
            rhobar = -cosine * alphas[step + 1]
            search = [-(theta / rho * s) for s in search] + [one]
    scale = [jnp.broadcast_to(u / a, (CC, 128)) for u, a in zip(update, alphas)]
    core = lax.axis_index("off")
    for refs_in, half in ((mine, core), (theirs, 1 - core)):
        at = pl.ds(pl.multiple_of(half * CC, CC), CC)
        for t in range(BLK_DEV // 128):
            cols = slice(t * 128, (t + 1) * 128)
            total = refs_in[0][:, cols] * scale[0]
            for i in range(1, ITERS):
                total = total + refs_in[i][:, cols] * scale[i]
            update_ref[at, cols] = total


def end_call(norm, q, mine, theirs, alphas, betas):
    return pl.pallas_call(
        end_kernel,
        out_shape=(
            jax.ShapeDtypeStruct((CELLS, BLK_DEV), F32),
            jax.ShapeDtypeStruct((RT, 128), F32),
        ),
        compiler_params=pltpu.CompilerParams(vmem_limit_bytes=8 << 20),
        name="end",
    )(norm, q, *mine, *theirs, *alphas, *betas)


def exchange(x):
    rest = x.shape[0] // SRC
    y = lax.all_to_all(x.reshape(SRC, rest, 128), ("win", "off"), 0, 0, tiled=True)
    return y.reshape(x.shape)


def body(kernels, blocks, counts, ray_of, slopes):
    ray = ray_of.reshape(N_WIN, CAP)
    q = slopes.reshape(RT, 128)
    k = start_call(
        kernels.reshape(SRC, CC, CAP), blocks.reshape(N_WIN, CAP), counts.reshape(1, N_WIN), ray, q
    )
    k = lax.all_to_all(k, ("win", "off"), 0, 0, tiled=True)
    mine, theirs, alphas, betas = [], [], [], []
    for step in range(ITERS):
        if step == 0:
            prev, vals, beta, ids, oh = owner_call(True, k)
        else:
            prev, vals, beta = owner_call(False, k, oh, ids, weights, prev, alpha)
        mine.append(prev)
        theirs.append(lax.ppermute(prev, "off", [(0, 1), (1, 0)]))
        betas.append(beta)
        weights, q, alpha, norm = window_call(exchange(vals), ray, q, beta)
        alphas.append(alpha)
        weights = exchange(weights)
    owner_call(False, k, oh, ids, weights, prev, alpha)
    update, data = end_call(exchange(norm), q, mine, theirs, alphas, betas)
    return update, data.reshape(1, 1, RAYS)


def solution(mesh):
    in_specs = (
        P("off", "win", None, None, None),
        P("off", "win", None, None),
        P("off", "win", None),
        P("off", "win", None, None),
        P("off", "win", None),
    )
    out_specs = (P(None, "win"), P("off", "win", None))
    return jax.shard_map(body, mesh=mesh, in_specs=in_specs, out_specs=out_specs, check_vma=False)
```

```python
import functools

import jax
import jax.numpy as jnp
from jax import lax
from jax.experimental import pallas as pl
from jax.experimental.pallas import tpu as pltpu
from jax.sharding import PartitionSpec as P

CELLS = 64
CAP = 128
BLK_DEV = 2048
RAYS = 512
ITERS = 3
N_OFF = 2
N_WIN = 64
SRC = N_OFF * N_WIN
CC = CELLS // N_OFF
RT = RAYS // 128
HI = 8
LO = BLK_DEV // HI
CA = 16
CF = 8
SLAB = CC + 4
F32 = jnp.float32
BF16 = jnp.bfloat16


def rows(ref, start, count, stride):
    return ref[pl.ds(start, count, stride=stride), :]


def ray_values(data, ray):
    lo = jnp.bitwise_and(ray, 127)
    hi = jnp.right_shift(ray, 7)
    parts = []
    for g in range(N_WIN // 8):
        lo_g, hi_g = lo[g * 8 : g * 8 + 8], hi[g * 8 : g * 8 + 8]
        acc = jnp.zeros((8, 128), F32)
        for t in range(RT):
            table = jnp.broadcast_to(data[t : t + 1], (8, 128))
            got = jnp.take_along_axis(table, lo_g, axis=1, mode="promise_in_bounds")
            acc = jnp.where(hi_g == t, got, acc)
        parts.append(acc)
    return jnp.concatenate(parts, axis=0)


def start_kernel(k_ref, blocks_in, counts_in, ray_in, slopes_in, out_ref, *scratch):
    blocks_ref, counts_ref, ray_ref, slopes_ref, extra_ref, sems = scratch
    rows_out = pltpu.make_async_copy(k_ref, out_ref.at[:, 0 : CC // 4], sems.at[0])
    rows_out.start()
    loads = [
        pltpu.make_async_copy(src, dst, sems.at[2 + n])
        for n, (src, dst) in enumerate(
            ((blocks_in, blocks_ref), (counts_in, counts_ref), (ray_in, ray_ref), (slopes_in, slopes_ref))
        )
    ]
    for load in loads:
        load.start()
    for load in loads:
        load.wait()
    slot = lax.broadcasted_iota(jnp.int32, (N_WIN, CAP), 1)
    row = lax.broadcasted_iota(jnp.int32, (N_WIN, N_WIN), 0)
    col = lax.broadcasted_iota(jnp.int32, (N_WIN, N_WIN), 1)
    counts = jnp.broadcast_to(counts_ref[...].astype(F32), (N_WIN, N_WIN))
    counts = jnp.sum(jnp.where(row == col, counts, 0.0), axis=1, keepdims=True)
    ids = jnp.where(slot.astype(F32) < counts, blocks_ref[...].astype(F32), -1.0)
    data = slopes_ref[...]
    weights = ray_values(data, ray_ref[...])
    part = jnp.full((N_WIN, 128), jnp.sum(data * data), F32)
    for h in range(N_OFF):
        for r, value in enumerate((ids, weights, part, part)):
            extra_ref[:, h, r, :] = value
    extra_out = pltpu.make_async_copy(
        extra_ref.reshape(SRC, 4, 128), out_ref.at[:, CC // 4], sems.at[1]
    )
    extra_out.start()
    rows_out.wait()
    extra_out.wait()


def start_call(k, blocks, counts, ray, slopes):
    return pl.pallas_call(
        start_kernel,
        out_shape=jax.ShapeDtypeStruct((SRC, SLAB // 4, 4, 128), F32),
        in_specs=[pl.BlockSpec(memory_space=pltpu.HBM)] * 5,
        out_specs=pl.BlockSpec(memory_space=pltpu.HBM),
        scratch_shapes=[
            pltpu.VMEM((N_WIN, CAP), jnp.int32),
            pltpu.VMEM((1, N_WIN), jnp.int32),
            pltpu.VMEM((N_WIN, CAP), jnp.int32),
            pltpu.VMEM((RT, 128), F32),
            pltpu.VMEM((N_WIN, N_OFF, 4, 128), F32),
            pltpu.SemaphoreType.DMA((6,)),
        ],
        compiler_params=pltpu.CompilerParams(vmem_limit_bytes=4 << 20),
        name="start",
    )(*(pltpu.with_memory_space_constraint(x, pltpu.HBM) for x in (k, blocks, counts, ray, slopes)))


def owner_kernel(first, k_ref, *refs):
    if first:
        p_ref, vals_ref, beta_ref, ids_ref, *scratch = refs
        ids_ref[...] = rows(k_ref, CC, SRC, SLAB).astype(jnp.int32)
        norms = rows(k_ref, CC + 2, SRC, SLAB)
        weight_of = lambda s: k_ref[pl.ds(SLAB * s + CC + 1, 1), :]
    else:
        ids_ref, wts_ref, pprev_ref, aprev_ref, p_ref, vals_ref, beta_ref, *scratch = refs
        norms = rows(wts_ref, 1, SRC, 2)
        weight_of = lambda s: wts_ref[pl.ds(2 * s, 1), :]
    oh_ref, y0_ref, y1_ref, acc_ref, v_ref, g0_ref, g1_ref = scratch
    steps = SRC // CA
    beta = jnp.sqrt(jnp.sum(norms, axis=0, keepdims=True))
    beta_ref[...] = beta
    acc_ref[...] = jnp.zeros_like(acc_ref)
    lo_iota = lax.broadcasted_iota(jnp.int32, (LO, 128), 0).astype(F32).astype(BF16)

    def spread(y_ref, i):
        for c in range(CA):
            s = i * CA + c
            at = slice(c * 128, (c + 1) * 128)
            blk = ids_ref[pl.ds(s, 1), :]
            hi = jnp.right_shift(blk, 8)
            lo = jnp.where(blk < 0, -1, jnp.bitwise_and(blk, LO - 1)).astype(F32)
            hit = lo_iota == jnp.broadcast_to(lo, (LO, 128)).astype(BF16)
            oh_ref[:, pl.ds(pl.multiple_of(s * 128, 128), 128)] = jnp.where(
                hit, jnp.ones((LO, 128), BF16), jnp.zeros((LO, 128), BF16)
            )
            x = k_ref[pl.ds(SLAB * s, CC), :] * jnp.broadcast_to(weight_of(s), (CC, 128))
            x1 = x.astype(BF16)
            x2 = (x - x1.astype(F32)).astype(BF16)
            hib = jnp.broadcast_to(hi.astype(F32), (CC, 128)).astype(BF16)
            zero = jnp.zeros((CC, 128), BF16)
            for h in range(HI):
                m = hib == jnp.asarray(h, BF16)
                y_ref[2 * h * CC : (2 * h + 1) * CC, at] = jnp.where(m, x1, zero)
                y_ref[(2 * h + 1) * CC : (2 * h + 2) * CC, at] = jnp.where(m, x2, zero)

    def add(y_ref, i):
        oh = oh_ref[:, pl.ds(pl.multiple_of(i * CA * 128, CA * 128), CA * 128)]
        acc_ref[...] += lax.dot_general(
            y_ref[...], oh, (((1,), (1,)), ((), ())), preferred_element_type=F32
        )

    def add_two(t, carry):
        add(y0_ref, 2 * t)
        spread(y1_ref, 2 * t + 1)
        add(y1_ref, 2 * t + 1)
        spread(y0_ref, 2 * t + 2)
        return carry

    steps = SRC // CA
    spread(y0_ref, 0)
    lax.fori_loop(0, steps // 2 - 1, add_two, 0)
    add(y0_ref, steps - 2)
    spread(y1_ref, steps - 1)
    add(y1_ref, steps - 1)

    squares = jnp.zeros((8, 128), F32)
    beta_b = jnp.broadcast_to(beta, (CC, 128))
    if not first:
        back = jnp.broadcast_to(beta / aprev_ref[...], (CC, 128))
    for h in range(HI):
        for t in range(LO // 128):
            at = slice(t * 128, (t + 1) * 128)
            g = acc_ref[2 * h * CC : (2 * h + 1) * CC, at] + acc_ref[(2 * h + 1) * CC : (2 * h + 2) * CC, at]
            g = g / beta_b
            cols = slice(h * LO + t * 128, h * LO + (t + 1) * 128)
            if not first:
                g = g - pprev_ref[:, cols] * back
            p_ref[:, cols] = g
            g1 = g.astype(BF16)
            v_ref[h * CC : (h + 1) * CC, at] = g1
            v_ref[(HI + h) * CC : (HI + h + 1) * CC, at] = (g - g1.astype(F32)).astype(BF16)
            g2 = g * g
            squares = squares + g2[0:8] + g2[8:16] + g2[16:24] + g2[24:32]
    vals_ref[pl.ds(1, SRC, stride=2), :] = jnp.full((SRC, 128), jnp.sum(squares), F32)

    def fetch(g_ref, i):
        oh = oh_ref[:, pl.ds(pl.multiple_of(i * CF * 128, CF * 128), CF * 128)]
        g_ref[...] = lax.dot_general(v_ref[...], oh, (((1,), (0,)), ((), ())), preferred_element_type=F32)

    def use(g_ref, i):
        for c in range(CF):
            s = i * CF + c
            at = slice(c * 128, (c + 1) * 128)
            hi = jnp.broadcast_to(jnp.right_shift(ids_ref[pl.ds(s, 1), :], 8), (8, 128))
            ks = [k_ref[pl.ds(SLAB * s + j, 8), :] for j in range(0, CC, 8)]
            total = jnp.zeros((8, 128), F32)
            for h in range(HI):
                part = None
                for j, kj in zip(range(0, CC, 8), ks):
                    r = h * CC + j
                    e = (g_ref[r : r + 8, at] + g_ref[HI * CC + r : HI * CC + r + 8, at]) * kj
                    part = e if part is None else part + e
                total = jnp.where(hi == h, part, total)
            vals_ref[pl.ds(2 * s, 1), :] = jnp.sum(total, axis=0, keepdims=True)

    def fetch_two(t, carry):
        fetch(g1_ref, 2 * t + 1)
        use(g0_ref, 2 * t)
        fetch(g0_ref, 2 * t + 2)
        use(g1_ref, 2 * t + 1)
        return carry

    last = SRC // CF - 1
    fetch(g0_ref, 0)
    lax.fori_loop(0, last // 2, fetch_two, 0)
    fetch(g1_ref, last)
    use(g0_ref, last - 1)
    use(g1_ref, last)


def owner_call(first, *args):
    outs = [
        jax.ShapeDtypeStruct((CC, BLK_DEV), F32),
        jax.ShapeDtypeStruct((2 * SRC, 128), F32),
        jax.ShapeDtypeStruct((1, 128), F32),
    ]
    if first:
        outs.append(jax.ShapeDtypeStruct((SRC, 128), jnp.int32))
    return pl.pallas_call(
        functools.partial(owner_kernel, first),
        out_shape=tuple(outs),
        scratch_shapes=[
            pltpu.VMEM((LO, SRC * 128), BF16),
            pltpu.VMEM((2 * HI * CC, CA * 128), BF16),
            pltpu.VMEM((2 * HI * CC, CA * 128), BF16),
            pltpu.VMEM((2 * HI * CC, LO), F32),
            pltpu.VMEM((2 * HI * CC, LO), BF16),
            pltpu.VMEM((2 * HI * CC, CF * 128), F32),
            pltpu.VMEM((2 * HI * CC, CF * 128), F32),
        ],
        compiler_params=pltpu.CompilerParams(vmem_limit_bytes=32 << 20),
        name="owner",
    )(*args)


def window_kernel(vals_ref, ray_ref, q_ref, beta_ref, wts_ref, qout_ref, alpha_ref, norm_ref, a_ref, b_ref):
    alpha = jnp.sqrt(jnp.sum(rows(vals_ref, 1, SRC, 2), axis=0, keepdims=True))
    alpha_ref[...] = alpha
    vals = rows(vals_ref, 0, N_WIN, 4) + rows(vals_ref, 2, N_WIN, 4)
    v1 = vals.astype(BF16).astype(F32)
    v2 = (vals - v1).astype(BF16).astype(F32)
    v3 = vals - v1 - v2
    ray = ray_ref[...]
    lo = jnp.bitwise_and(ray, 127)
    hi = jnp.right_shift(ray, 7)
    sub = lax.broadcasted_iota(jnp.int32, (8, 128), 0)
    tier = jnp.bitwise_and(sub, RT - 1)
    lo_iota = lax.broadcasted_iota(jnp.int32, (128, 128), 0)
    wide = lambda r, p, n: jnp.broadcast_to(r[p : p + 1], (n, 128))
    for p in range(N_WIN):
        at = slice(p * 128, (p + 1) * 128)
        hit = tier == wide(hi, p, 8)
        upper = jnp.where(sub < RT, wide(v1, p, 8), wide(v2, p, 8))
        lower = jnp.where(sub < RT, wide(v3, p, 8), 0.0)
        both = jnp.concatenate([jnp.where(hit, upper, 0.0), jnp.where(hit, lower, 0.0)], axis=0)
        a_ref[:, at] = both.astype(BF16)
        b_ref[:, at] = jnp.where(lo_iota == wide(lo, p, 128), 1.0, 0.0).astype(BF16)
    out = lax.dot_general(a_ref[...], b_ref[...], (((1,), (1,)), ((), ())), preferred_element_type=F32)
    summed = out[0:RT] + out[RT : 2 * RT] + out[2 * RT : 3 * RT]
    alpha_b = jnp.broadcast_to(alpha, (RT, 128))
    beta_b = jnp.broadcast_to(beta_ref[...], (RT, 128))
    q = summed / alpha_b - alpha_b * (q_ref[...] / beta_b)
    qout_ref[...] = q
    part = jnp.sum(q * q)
    weights = ray_values(q, ray)
    wts_ref[pl.ds(0, N_WIN, stride=4), :] = weights
    wts_ref[pl.ds(2, N_WIN, stride=4), :] = weights
    wts_ref[pl.ds(1, SRC, stride=2), :] = jnp.full((SRC, 128), part, F32)
    norm_ref[...] = jnp.full((SRC, 128), part, F32)


def window_call(vals, ray, q, beta):
    return pl.pallas_call(
        window_kernel,
        out_shape=(
            jax.ShapeDtypeStruct((2 * SRC, 128), F32),
            jax.ShapeDtypeStruct((RT, 128), F32),
            jax.ShapeDtypeStruct((1, 128), F32),
            jax.ShapeDtypeStruct((SRC, 128), F32),
        ),
        scratch_shapes=[
            pltpu.VMEM((16, N_WIN * 128), BF16),
            pltpu.VMEM((128, N_WIN * 128), BF16),
        ],
        compiler_params=pltpu.CompilerParams(vmem_limit_bytes=8 << 20),
        name="window",
    )(vals, ray, q, beta)


def end_kernel(norm_ref, q_ref, *refs):
    mine, theirs = refs[0:ITERS], refs[ITERS : 2 * ITERS]
    alphas = [r[...] for r in refs[2 * ITERS : 3 * ITERS]]
    betas = [r[...] for r in refs[3 * ITERS : 4 * ITERS]]
    update_ref, data_ref = refs[4 * ITERS :]
    betas.append(jnp.sqrt(jnp.sum(norm_ref[...], axis=0, keepdims=True)))
    data_ref[...] = q_ref[...] / jnp.broadcast_to(betas[ITERS], (RT, 128))
    one = jnp.ones_like(alphas[0])
    phibar, rhobar = betas[0], alphas[0]
    search = [one]
    update = [jnp.zeros_like(one) for _ in range(ITERS)]
    for step in range(ITERS):
        beta = betas[step + 1]
        rho = jnp.sqrt(rhobar * rhobar + beta * beta)
        cosine = rhobar / rho
        sine = beta / rho
        phi = cosine * phibar
        phibar = sine * phibar
        for i, s in enumerate(search):
            update[i] = update[i] + phi / rho * s
        if step + 1 < ITERS:
            theta = sine * alphas[step + 1]
            rhobar = -cosine * alphas[step + 1]
            search = [-(theta / rho * s) for s in search] + [one]
    scale = [jnp.broadcast_to(u / a, (CC, 128)) for u, a in zip(update, alphas)]
    core = lax.axis_index("off")
    for refs_in, half in ((mine, core), (theirs, 1 - core)):
        at = pl.ds(pl.multiple_of(half * CC, CC), CC)
        for t in range(BLK_DEV // 128):
            cols = slice(t * 128, (t + 1) * 128)
            total = refs_in[0][:, cols] * scale[0]
            for i in range(1, ITERS):
                total = total + refs_in[i][:, cols] * scale[i]
            update_ref[at, cols] = total


def end_call(norm, q, mine, theirs, alphas, betas):
    return pl.pallas_call(
        end_kernel,
        out_shape=(
            jax.ShapeDtypeStruct((CELLS, BLK_DEV), F32),
            jax.ShapeDtypeStruct((RT, 128), F32),
        ),
        compiler_params=pltpu.CompilerParams(vmem_limit_bytes=8 << 20),
        name="end",
    )(norm, q, *mine, *theirs, *alphas, *betas)


def exchange(x):
    rest = x.shape[0] // SRC
    y = lax.all_to_all(x.reshape(SRC, rest, 128), ("win", "off"), 0, 0, tiled=True)
    return y.reshape(x.shape)


def body(kernels, blocks, counts, ray_of, slopes):
    ray = ray_of.reshape(N_WIN, CAP)
    q = slopes.reshape(RT, 128)
    k = start_call(
        kernels.reshape(SRC, CC // 4, 4, CAP), blocks.reshape(N_WIN, CAP), counts.reshape(1, N_WIN), ray, q
    )
    k = lax.all_to_all(k, ("win", "off"), 0, 0, tiled=True).reshape(SRC * SLAB, CAP)
    mine, theirs, alphas, betas = [], [], [], []
    for step in range(ITERS):
        if step == 0:
            prev, vals, beta, ids = owner_call(True, k)
        else:
            prev, vals, beta = owner_call(False, k, ids, weights, prev, alpha)
        mine.append(prev)
        theirs.append(lax.ppermute(prev, "off", [(0, 1), (1, 0)]))
        betas.append(beta)
        weights, q, alpha, norm = window_call(exchange(vals), ray, q, beta)
        alphas.append(alpha)
        weights = exchange(weights)
    owner_call(False, k, ids, weights, prev, alpha)
    update, data = end_call(exchange(norm), q, mine, theirs, alphas, betas)
    return update, data.reshape(1, 1, RAYS)


def solution(mesh):
    in_specs = (
        P("off", "win", None, None, None),
        P("off", "win", None, None),
        P("off", "win", None),
        P("off", "win", None, None),
        P("off", "win", None),
    )
    out_specs = (P(None, "win"), P("off", "win", None))
    return jax.shard_map(body, mesh=mesh, in_specs=in_specs, out_specs=out_specs, check_vma=False)
```

```python
import functools

import jax
import jax.numpy as jnp
from jax import lax
from jax.experimental import pallas as pl
from jax.experimental.pallas import tpu as pltpu
from jax.sharding import PartitionSpec as P

CELLS = 64
CAP = 128
BLK_DEV = 2048
RAYS = 512
ITERS = 3
N_OFF = 2
N_WIN = 64
SRC = N_OFF * N_WIN
CC = CELLS // N_OFF
RT = RAYS // 128
HI = 8
LO = BLK_DEV // HI
CA = 16
MC = 24
CF = 8
SLAB = CC + 4
F32 = jnp.float32
BF16 = jnp.bfloat16


def rows(ref, start, count, stride):
    return ref[pl.ds(start, count, stride=stride), :]


def ray_values(data, ray):
    lo = jnp.bitwise_and(ray, 127)
    hi = jnp.right_shift(ray, 7)
    parts = []
    for g in range(N_WIN // 8):
        lo_g, hi_g = lo[g * 8 : g * 8 + 8], hi[g * 8 : g * 8 + 8]
        acc = jnp.zeros((8, 128), F32)
        for t in range(RT):
            table = jnp.broadcast_to(data[t : t + 1], (8, 128))
            got = jnp.take_along_axis(table, lo_g, axis=1, mode="promise_in_bounds")
            acc = jnp.where(hi_g == t, got, acc)
        parts.append(acc)
    return jnp.concatenate(parts, axis=0)


def start_kernel(k_ref, blocks_in, counts_in, ray_in, slopes_in, out_ref, *scratch):
    blocks_ref, counts_ref, ray_ref, slopes_ref, extra_ref, sems = scratch
    rows_out = pltpu.make_async_copy(k_ref, out_ref.at[:, 0 : CC // 4], sems.at[0])
    rows_out.start()
    loads = [
        pltpu.make_async_copy(src, dst, sems.at[2 + n])
        for n, (src, dst) in enumerate(
            ((blocks_in, blocks_ref), (counts_in, counts_ref), (ray_in, ray_ref), (slopes_in, slopes_ref))
        )
    ]
    for load in loads:
        load.start()
    for load in loads:
        load.wait()
    slot = lax.broadcasted_iota(jnp.int32, (N_WIN, CAP), 1)
    row = lax.broadcasted_iota(jnp.int32, (N_WIN, N_WIN), 0)
    col = lax.broadcasted_iota(jnp.int32, (N_WIN, N_WIN), 1)
    counts = jnp.broadcast_to(counts_ref[...].astype(F32), (N_WIN, N_WIN))
    counts = jnp.sum(jnp.where(row == col, counts, 0.0), axis=1, keepdims=True)
    ids = jnp.where(slot.astype(F32) < counts, blocks_ref[...].astype(F32), -1.0)
    data = slopes_ref[...]
    weights = ray_values(data, ray_ref[...])
    part = jnp.full((N_WIN, 128), jnp.sum(data * data), F32)
    for h in range(N_OFF):
        for r, value in enumerate((ids, weights, part, part)):
            extra_ref[:, h, r, :] = value
    extra_out = pltpu.make_async_copy(
        extra_ref.reshape(SRC, 4, 128), out_ref.at[:, CC // 4], sems.at[1]
    )
    extra_out.start()
    rows_out.wait()
    extra_out.wait()


def start_call(k, blocks, counts, ray, slopes):
    return pl.pallas_call(
        start_kernel,
        out_shape=jax.ShapeDtypeStruct((SRC, SLAB // 4, 4, 128), F32),
        in_specs=[pl.BlockSpec(memory_space=pltpu.HBM)] * 5,
        out_specs=pl.BlockSpec(memory_space=pltpu.HBM),
        scratch_shapes=[
            pltpu.VMEM((N_WIN, CAP), jnp.int32),
            pltpu.VMEM((1, N_WIN), jnp.int32),
            pltpu.VMEM((N_WIN, CAP), jnp.int32),
            pltpu.VMEM((RT, 128), F32),
            pltpu.VMEM((N_WIN, N_OFF, 4, 128), F32),
            pltpu.SemaphoreType.DMA((6,)),
        ],
        compiler_params=pltpu.CompilerParams(vmem_limit_bytes=4 << 20),
        name="start",
    )(*(pltpu.with_memory_space_constraint(x, pltpu.HBM) for x in (k, blocks, counts, ray, slopes)))


def owner_kernel(first, k_ref, *refs):
    if first:
        p_ref, vals_ref, beta_ref, ids_ref, *scratch = refs
        ids_ref[...] = rows(k_ref, CC, SRC, SLAB).astype(jnp.int32)
        norms = rows(k_ref, CC + 2, SRC, SLAB)
        weight_of = lambda s: k_ref[pl.ds(SLAB * s + CC + 1, 1), :]
    else:
        ids_ref, wts_ref, pprev_ref, aprev_ref, p_ref, vals_ref, beta_ref, *scratch = refs
        norms = rows(wts_ref, 1, SRC, 2)
        weight_of = lambda s: wts_ref[pl.ds(2 * s, 1), :]
    oh_ref, y0_ref, y1_ref, acc_ref, v_ref, g0_ref, g1_ref = scratch
    steps = SRC // CA
    beta = jnp.sqrt(jnp.sum(norms, axis=0, keepdims=True))
    beta_ref[...] = beta
    acc_ref[...] = jnp.zeros_like(acc_ref)
    lo_iota = lax.broadcasted_iota(jnp.int32, (LO, 128), 0).astype(F32).astype(BF16)

    def spread(y_ref, i):
        for c in range(CA):
            s = i * CA + c
            at = slice(c * 128, (c + 1) * 128)
            blk = ids_ref[pl.ds(s, 1), :]
            hi = jnp.right_shift(blk, 8)
            lo = jnp.where(blk < 0, -1, jnp.bitwise_and(blk, LO - 1)).astype(F32)
            hit = lo_iota == jnp.broadcast_to(lo, (LO, 128)).astype(BF16)
            oh_ref[:, pl.ds(pl.multiple_of(s * 128, 128), 128)] = jnp.where(
                hit, jnp.ones((LO, 128), BF16), jnp.zeros((LO, 128), BF16)
            )
            x = k_ref[pl.ds(SLAB * s, CC), :] * jnp.broadcast_to(weight_of(s), (CC, 128))
            x1 = x.astype(BF16)
            x2 = (x - x1.astype(F32)).astype(BF16)
            hib = jnp.broadcast_to(hi.astype(F32), (CC, 128)).astype(BF16)
            zero = jnp.zeros((CC, 128), BF16)
            for h in range(HI):
                m = hib == jnp.asarray(h, BF16)
                y_ref[2 * h * CC : (2 * h + 1) * CC, at] = jnp.where(m, x1, zero)
                y_ref[(2 * h + 1) * CC : (2 * h + 2) * CC, at] = jnp.where(m, x2, zero)

    def add(y_ref, i):
        oh = oh_ref[:, pl.ds(pl.multiple_of(i * CA * 128, CA * 128), CA * 128)]
        acc_ref[...] += lax.dot_general(
            y_ref[...], oh, (((1,), (1,)), ((), ())), preferred_element_type=F32
        )

    def add_two(t, carry):
        add(y0_ref, 2 * t)
        spread(y1_ref, 2 * t + 1)
        add(y1_ref, 2 * t + 1)
        spread(y0_ref, 2 * t + 2)
        return carry

    steps = SRC // CA
    spread(y0_ref, 0)
    lax.fori_loop(0, steps // 2 - 1, add_two, 0)
    add(y0_ref, steps - 2)
    spread(y1_ref, steps - 1)
    add(y1_ref, steps - 1)

    squares = jnp.zeros((8, 128), F32)
    beta_b = jnp.broadcast_to(beta, (CC, 128))
    if not first:
        back = jnp.broadcast_to(beta / aprev_ref[...], (CC, 128))
    for h in range(HI):
        for t in range(LO // 128):
            at = slice(t * 128, (t + 1) * 128)
            g = acc_ref[2 * h * CC : (2 * h + 1) * CC, at] + acc_ref[(2 * h + 1) * CC : (2 * h + 2) * CC, at]
            g = g / beta_b
            cols = slice(h * LO + t * 128, h * LO + (t + 1) * 128)
            if not first:
                g = g - pprev_ref[:, cols] * back
            p_ref[:, cols] = g
            gm = g[0:MC]
            g1 = gm.astype(BF16)
            v_ref[h * MC : (h + 1) * MC, at] = g1
            v_ref[(HI + h) * MC : (HI + h + 1) * MC, at] = (gm - g1.astype(F32)).astype(BF16)
            g2 = g * g
            squares = squares + g2[0:8] + g2[8:16] + g2[16:24] + g2[24:32]
    vals_ref[pl.ds(1, SRC, stride=2), :] = jnp.full((SRC, 128), jnp.sum(squares), F32)

    def fetch(g_ref, i):
        oh = oh_ref[:, pl.ds(pl.multiple_of(i * CF * 128, CF * 128), CF * 128)]
        g_ref[...] = lax.dot_general(v_ref[...], oh, (((1,), (0,)), ((), ())), preferred_element_type=F32)

    def use(g_ref, i):
        for c in range(CF):
            s = i * CF + c
            at = slice(c * 128, (c + 1) * 128)
            blk = jnp.broadcast_to(ids_ref[pl.ds(s, 1), :], (8, 128))
            hi = jnp.right_shift(blk, 8)
            ks = [k_ref[pl.ds(SLAB * s + j, 8), :] for j in range(0, CC, 8)]
            total = jnp.zeros((8, 128), F32)
            for h in range(HI):
                part = None
                for j, kj in zip(range(0, MC, 8), ks):
                    r = h * MC + j
                    e = (g_ref[r : r + 8, at] + g_ref[HI * MC + r : HI * MC + r + 8, at]) * kj
                    part = e if part is None else part + e
                total = jnp.where(hi == h, part, total)
            lo7 = jnp.bitwise_and(blk, 127)
            hi7 = jnp.right_shift(blk, 7)
            for j, kj in zip(range(MC, CC, 8), ks[MC // 8 :]):
                value = jnp.zeros((8, 128), F32)
                for h in range(BLK_DEV // 128):
                    table = p_ref[j : j + 8, h * 128 : (h + 1) * 128]
                    got = jnp.take_along_axis(table, lo7, axis=1, mode="promise_in_bounds")
                    value = jnp.where(hi7 == h, got, value)
                total = total + value * kj
            vals_ref[pl.ds(2 * s, 1), :] = jnp.sum(total, axis=0, keepdims=True)

    def fetch_two(t, carry):
        fetch(g1_ref, 2 * t + 1)
        use(g0_ref, 2 * t)
        fetch(g0_ref, 2 * t + 2)
        use(g1_ref, 2 * t + 1)
        return carry

    last = SRC // CF - 1
    fetch(g0_ref, 0)
    lax.fori_loop(0, last // 2, fetch_two, 0)
    fetch(g1_ref, last)
    use(g0_ref, last - 1)
    use(g1_ref, last)


def owner_call(first, *args):
    outs = [
        jax.ShapeDtypeStruct((CC, BLK_DEV), F32),
        jax.ShapeDtypeStruct((2 * SRC, 128), F32),
        jax.ShapeDtypeStruct((1, 128), F32),
    ]
    if first:
        outs.append(jax.ShapeDtypeStruct((SRC, 128), jnp.int32))
    return pl.pallas_call(
        functools.partial(owner_kernel, first),
        out_shape=tuple(outs),
        scratch_shapes=[
            pltpu.VMEM((LO, SRC * 128), BF16),
            pltpu.VMEM((2 * HI * CC, CA * 128), BF16),
            pltpu.VMEM((2 * HI * CC, CA * 128), BF16),
            pltpu.VMEM((2 * HI * CC, LO), F32),
            pltpu.VMEM((2 * HI * MC, LO), BF16),
            pltpu.VMEM((2 * HI * MC, CF * 128), F32),
            pltpu.VMEM((2 * HI * MC, CF * 128), F32),
        ],
        compiler_params=pltpu.CompilerParams(vmem_limit_bytes=32 << 20),
        name="owner",
    )(*args)


def window_kernel(vals_ref, ray_ref, q_ref, beta_ref, wts_ref, qout_ref, alpha_ref, norm_ref, a_ref, b_ref):
    alpha = jnp.sqrt(jnp.sum(rows(vals_ref, 1, SRC, 2), axis=0, keepdims=True))
    alpha_ref[...] = alpha
    vals = rows(vals_ref, 0, N_WIN, 4) + rows(vals_ref, 2, N_WIN, 4)
    v1 = vals.astype(BF16).astype(F32)
    v2 = (vals - v1).astype(BF16).astype(F32)
    v3 = vals - v1 - v2
    ray = ray_ref[...]
    lo = jnp.bitwise_and(ray, 127).astype(F32)
    hi = jnp.right_shift(ray, 7)
    sub = lax.broadcasted_iota(jnp.int32, (8, 128), 0)
    tier = jnp.bitwise_and(sub, RT - 1)
    lo_iota = lax.broadcasted_iota(jnp.int32, (128, 128), 0).astype(F32).astype(BF16)
    ones, zeros = jnp.ones((128, 128), BF16), jnp.zeros((128, 128), BF16)
    wide = lambda r, p, n: jnp.broadcast_to(r[p : p + 1], (n, 128))
    for p in range(N_WIN):
        at = slice(p * 128, (p + 1) * 128)
        hit = tier == wide(hi, p, 8)
        upper = jnp.where(sub < RT, wide(v1, p, 8), wide(v2, p, 8))
        lower = jnp.where(sub < RT, wide(v3, p, 8), 0.0)
        both = jnp.concatenate([jnp.where(hit, upper, 0.0), jnp.where(hit, lower, 0.0)], axis=0)
        a_ref[:, at] = both.astype(BF16)
        b_ref[:, at] = jnp.where(lo_iota == wide(lo, p, 128).astype(BF16), ones, zeros)
    out = lax.dot_general(a_ref[...], b_ref[...], (((1,), (1,)), ((), ())), preferred_element_type=F32)
    summed = out[0:RT] + out[RT : 2 * RT] + out[2 * RT : 3 * RT]
    alpha_b = jnp.broadcast_to(alpha, (RT, 128))
    beta_b = jnp.broadcast_to(beta_ref[...], (RT, 128))
    q = summed / alpha_b - alpha_b * (q_ref[...] / beta_b)
    qout_ref[...] = q
    part = jnp.sum(q * q)
    weights = ray_values(q, ray)
    wts_ref[pl.ds(0, N_WIN, stride=4), :] = weights
    wts_ref[pl.ds(2, N_WIN, stride=4), :] = weights
    wts_ref[pl.ds(1, SRC, stride=2), :] = jnp.full((SRC, 128), part, F32)
    norm_ref[...] = jnp.full((SRC, 128), part, F32)


def window_call(vals, ray, q, beta):
    return pl.pallas_call(
        window_kernel,
        out_shape=(
            jax.ShapeDtypeStruct((2 * SRC, 128), F32),
            jax.ShapeDtypeStruct((RT, 128), F32),
            jax.ShapeDtypeStruct((1, 128), F32),
            jax.ShapeDtypeStruct((SRC, 128), F32),
        ),
        scratch_shapes=[
            pltpu.VMEM((16, N_WIN * 128), BF16),
            pltpu.VMEM((128, N_WIN * 128), BF16),
        ],
        compiler_params=pltpu.CompilerParams(vmem_limit_bytes=8 << 20),
        name="window",
    )(vals, ray, q, beta)


def end_kernel(norm_ref, q_ref, *refs):
    mine, theirs = refs[0:ITERS], refs[ITERS : 2 * ITERS]
    alphas = [r[...] for r in refs[2 * ITERS : 3 * ITERS]]
    betas = [r[...] for r in refs[3 * ITERS : 4 * ITERS]]
    update_ref, data_ref = refs[4 * ITERS :]
    betas.append(jnp.sqrt(jnp.sum(norm_ref[...], axis=0, keepdims=True)))
    data_ref[...] = q_ref[...] / jnp.broadcast_to(betas[ITERS], (RT, 128))
    one = jnp.ones_like(alphas[0])
    phibar, rhobar = betas[0], alphas[0]
    search = [one]
    update = [jnp.zeros_like(one) for _ in range(ITERS)]
    for step in range(ITERS):
        beta = betas[step + 1]
        rho = jnp.sqrt(rhobar * rhobar + beta * beta)
        cosine = rhobar / rho
        sine = beta / rho
        phi = cosine * phibar
        phibar = sine * phibar
        for i, s in enumerate(search):
            update[i] = update[i] + phi / rho * s
        if step + 1 < ITERS:
            theta = sine * alphas[step + 1]
            rhobar = -cosine * alphas[step + 1]
            search = [-(theta / rho * s) for s in search] + [one]
    scale = [jnp.broadcast_to(u / a, (CC, 128)) for u, a in zip(update, alphas)]
    core = lax.axis_index("off")
    for refs_in, half in ((mine, core), (theirs, 1 - core)):
        at = pl.ds(pl.multiple_of(half * CC, CC), CC)
        for t in range(BLK_DEV // 128):
            cols = slice(t * 128, (t + 1) * 128)
            total = refs_in[0][:, cols] * scale[0]
            for i in range(1, ITERS):
                total = total + refs_in[i][:, cols] * scale[i]
            update_ref[at, cols] = total


def end_call(norm, q, mine, theirs, alphas, betas):
    return pl.pallas_call(
        end_kernel,
        out_shape=(
            jax.ShapeDtypeStruct((CELLS, BLK_DEV), F32),
            jax.ShapeDtypeStruct((RT, 128), F32),
        ),
        compiler_params=pltpu.CompilerParams(vmem_limit_bytes=8 << 20),
        name="end",
    )(norm, q, *mine, *theirs, *alphas, *betas)


def exchange(x):
    rest = x.shape[0] // SRC
    y = lax.all_to_all(x.reshape(SRC, rest, 128), ("win", "off"), 0, 0, tiled=True)
    return y.reshape(x.shape)


def body(kernels, blocks, counts, ray_of, slopes):
    ray = ray_of.reshape(N_WIN, CAP)
    q = slopes.reshape(RT, 128)
    k = start_call(
        kernels.reshape(SRC, CC // 4, 4, CAP), blocks.reshape(N_WIN, CAP), counts.reshape(1, N_WIN), ray, q
    )
    k = lax.all_to_all(k, ("win", "off"), 0, 0, tiled=True).reshape(SRC * SLAB, CAP)
    mine, theirs, alphas, betas = [], [], [], []
    for step in range(ITERS):
        if step == 0:
            prev, vals, beta, ids = owner_call(True, k)
        else:
            prev, vals, beta = owner_call(False, k, ids, weights, prev, alpha)
        mine.append(prev)
        theirs.append(lax.ppermute(prev, "off", [(0, 1), (1, 0)]))
        betas.append(beta)
        weights, q, alpha, norm = window_call(exchange(vals), ray, q, beta)
        alphas.append(alpha)
        weights = exchange(weights)
    owner_call(False, k, ids, weights, prev, alpha)
    update, data = end_call(exchange(norm), q, mine, theirs, alphas, betas)
    return update, data.reshape(1, 1, RAYS)


def solution(mesh):
    in_specs = (
        P("off", "win", None, None, None),
        P("off", "win", None, None),
        P("off", "win", None),
        P("off", "win", None, None),
        P("off", "win", None),
    )
    out_specs = (P(None, "win"), P("off", "win", None))
    return jax.shard_map(body, mesh=mesh, in_specs=in_specs, out_specs=out_specs, check_vma=False)
```

```python
import functools

import jax
import jax.numpy as jnp
from jax import lax
from jax.experimental import pallas as pl
from jax.experimental.pallas import tpu as pltpu
from jax.sharding import PartitionSpec as P

CELLS = 64
CAP = 128
BLK_DEV = 2048
RAYS = 512
ITERS = 3
N_OFF = 2
N_WIN = 64
SRC = N_OFF * N_WIN
CC = CELLS // N_OFF
RT = RAYS // 128
HI = 8
LO = BLK_DEV // HI
CA = 16
MC = 16
CF = 8
SLAB = CC + 4
F32 = jnp.float32
BF16 = jnp.bfloat16


def rows(ref, start, count, stride):
    return ref[pl.ds(start, count, stride=stride), :]


def ray_values(data, ray):
    lo = jnp.bitwise_and(ray, 127)
    hi = jnp.right_shift(ray, 7)
    parts = []
    for g in range(N_WIN // 8):
        lo_g, hi_g = lo[g * 8 : g * 8 + 8], hi[g * 8 : g * 8 + 8]
        acc = jnp.zeros((8, 128), F32)
        for t in range(RT):
            table = jnp.broadcast_to(data[t : t + 1], (8, 128))
            got = jnp.take_along_axis(table, lo_g, axis=1, mode="promise_in_bounds")
            acc = jnp.where(hi_g == t, got, acc)
        parts.append(acc)
    return jnp.concatenate(parts, axis=0)


def start_kernel(k_ref, blocks_in, counts_in, ray_in, slopes_in, out_ref, *scratch):
    blocks_ref, counts_ref, ray_ref, slopes_ref, extra_ref, sems = scratch
    rows_out = pltpu.make_async_copy(k_ref, out_ref.at[:, 0 : CC // 4], sems.at[0])
    rows_out.start()
    loads = [
        pltpu.make_async_copy(src, dst, sems.at[2 + n])
        for n, (src, dst) in enumerate(
            ((blocks_in, blocks_ref), (counts_in, counts_ref), (ray_in, ray_ref), (slopes_in, slopes_ref))
        )
    ]
    for load in loads:
        load.start()
    for load in loads:
        load.wait()
    slot = lax.broadcasted_iota(jnp.int32, (N_WIN, CAP), 1)
    row = lax.broadcasted_iota(jnp.int32, (N_WIN, N_WIN), 0)
    col = lax.broadcasted_iota(jnp.int32, (N_WIN, N_WIN), 1)
    counts = jnp.broadcast_to(counts_ref[...].astype(F32), (N_WIN, N_WIN))
    counts = jnp.sum(jnp.where(row == col, counts, 0.0), axis=1, keepdims=True)
    ids = jnp.where(slot.astype(F32) < counts, blocks_ref[...].astype(F32), -1.0)
    data = slopes_ref[...]
    weights = ray_values(data, ray_ref[...])
    part = jnp.full((N_WIN, 128), jnp.sum(data * data), F32)
    for h in range(N_OFF):
        for r, value in enumerate((ids, weights, part, part)):
            extra_ref[:, h, r, :] = value
    extra_out = pltpu.make_async_copy(
        extra_ref.reshape(SRC, 4, 128), out_ref.at[:, CC // 4], sems.at[1]
    )
    extra_out.start()
    rows_out.wait()
    extra_out.wait()


def start_call(k, blocks, counts, ray, slopes):
    return pl.pallas_call(
        start_kernel,
        out_shape=jax.ShapeDtypeStruct((SRC, SLAB // 4, 4, 128), F32),
        in_specs=[pl.BlockSpec(memory_space=pltpu.HBM)] * 5,
        out_specs=pl.BlockSpec(memory_space=pltpu.HBM),
        scratch_shapes=[
            pltpu.VMEM((N_WIN, CAP), jnp.int32),
            pltpu.VMEM((1, N_WIN), jnp.int32),
            pltpu.VMEM((N_WIN, CAP), jnp.int32),
            pltpu.VMEM((RT, 128), F32),
            pltpu.VMEM((N_WIN, N_OFF, 4, 128), F32),
            pltpu.SemaphoreType.DMA((6,)),
        ],
        compiler_params=pltpu.CompilerParams(vmem_limit_bytes=4 << 20),
        name="start",
    )(*(pltpu.with_memory_space_constraint(x, pltpu.HBM) for x in (k, blocks, counts, ray, slopes)))


def owner_kernel(first, k_ref, *refs):
    if first:
        p_ref, vals_ref, beta_ref, ids_ref, *scratch = refs
        ids_ref[...] = rows(k_ref, CC, SRC, SLAB).astype(jnp.int32)
        norms = rows(k_ref, CC + 2, SRC, SLAB)
        weight_of = lambda s: k_ref[pl.ds(SLAB * s + CC + 1, 1), :]
    else:
        ids_ref, wts_ref, pprev_ref, aprev_ref, p_ref, vals_ref, beta_ref, *scratch = refs
        norms = rows(wts_ref, 1, SRC, 2)
        weight_of = lambda s: wts_ref[pl.ds(2 * s, 1), :]
    oh_ref, y0_ref, y1_ref, acc_ref, v_ref, g0_ref, g1_ref = scratch
    steps = SRC // CA
    beta = jnp.sqrt(jnp.sum(norms, axis=0, keepdims=True))
    beta_ref[...] = beta
    acc_ref[...] = jnp.zeros_like(acc_ref)
    lo_iota = lax.broadcasted_iota(jnp.int32, (LO, 128), 0).astype(F32).astype(BF16)

    def spread(y_ref, i):
        for c in range(CA):
            s = i * CA + c
            at = slice(c * 128, (c + 1) * 128)
            blk = ids_ref[pl.ds(s, 1), :]
            hi = jnp.right_shift(blk, 8)
            lo = jnp.where(blk < 0, -1, jnp.bitwise_and(blk, LO - 1)).astype(F32)
            hit = lo_iota == jnp.broadcast_to(lo, (LO, 128)).astype(BF16)
            oh_ref[:, pl.ds(pl.multiple_of(s * 128, 128), 128)] = jnp.where(
                hit, jnp.ones((LO, 128), BF16), jnp.zeros((LO, 128), BF16)
            )
            x = k_ref[pl.ds(SLAB * s, CC), :] * jnp.broadcast_to(weight_of(s), (CC, 128))
            x1 = x.astype(BF16)
            x2 = (x - x1.astype(F32)).astype(BF16)
            hib = jnp.broadcast_to(hi.astype(F32), (CC, 128)).astype(BF16)
            zero = jnp.zeros((CC, 128), BF16)
            for h in range(HI):
                m = hib == jnp.asarray(h, BF16)
                y_ref[2 * h * CC : (2 * h + 1) * CC, at] = jnp.where(m, x1, zero)
                y_ref[(2 * h + 1) * CC : (2 * h + 2) * CC, at] = jnp.where(m, x2, zero)

    def add(y_ref, i):
        oh = oh_ref[:, pl.ds(pl.multiple_of(i * CA * 128, CA * 128), CA * 128)]
        acc_ref[...] += lax.dot_general(
            y_ref[...], oh, (((1,), (1,)), ((), ())), preferred_element_type=F32
        )

    def add_two(t, carry):
        add(y0_ref, 2 * t)
        spread(y1_ref, 2 * t + 1)
        add(y1_ref, 2 * t + 1)
        spread(y0_ref, 2 * t + 2)
        return carry

    steps = SRC // CA
    spread(y0_ref, 0)
    lax.fori_loop(0, steps // 2 - 1, add_two, 0)
    add(y0_ref, steps - 2)
    spread(y1_ref, steps - 1)
    add(y1_ref, steps - 1)

    squares = jnp.zeros((8, 128), F32)
    beta_b = jnp.broadcast_to(beta, (CC, 128))
    if not first:
        back = jnp.broadcast_to(beta / aprev_ref[...], (CC, 128))
    for h in range(HI):
        for t in range(LO // 128):
            at = slice(t * 128, (t + 1) * 128)
            g = acc_ref[2 * h * CC : (2 * h + 1) * CC, at] + acc_ref[(2 * h + 1) * CC : (2 * h + 2) * CC, at]
            g = g / beta_b
            cols = slice(h * LO + t * 128, h * LO + (t + 1) * 128)
            if not first:
                g = g - pprev_ref[:, cols] * back
            p_ref[:, cols] = g
            gm = g[0:MC]
            g1 = gm.astype(BF16)
            v_ref[h * MC : (h + 1) * MC, at] = g1
            v_ref[(HI + h) * MC : (HI + h + 1) * MC, at] = (gm - g1.astype(F32)).astype(BF16)
            g2 = g * g
            squares = squares + g2[0:8] + g2[8:16] + g2[16:24] + g2[24:32]
    vals_ref[pl.ds(1, SRC, stride=2), :] = jnp.full((SRC, 128), jnp.sum(squares), F32)

    def fetch(g_ref, i):
        oh = oh_ref[:, pl.ds(pl.multiple_of(i * CF * 128, CF * 128), CF * 128)]
        g_ref[...] = lax.dot_general(v_ref[...], oh, (((1,), (0,)), ((), ())), preferred_element_type=F32)

    def use(g_ref, i):
        for c in range(CF):
            s = i * CF + c
            at = slice(c * 128, (c + 1) * 128)
            blk = jnp.broadcast_to(ids_ref[pl.ds(s, 1), :], (8, 128))
            hi = jnp.right_shift(blk, 8)
            ks = [k_ref[pl.ds(SLAB * s + j, 8), :] for j in range(0, CC, 8)]
            total = jnp.zeros((8, 128), F32)
            for h in range(HI):
                part = None
                for j, kj in zip(range(0, MC, 8), ks):
                    r = h * MC + j
                    e = (g_ref[r : r + 8, at] + g_ref[HI * MC + r : HI * MC + r + 8, at]) * kj
                    part = e if part is None else part + e
                total = jnp.where(hi == h, part, total)
            lo7 = jnp.bitwise_and(blk, 127)
            hi7 = jnp.right_shift(blk, 7)
            for j, kj in zip(range(MC, CC, 8), ks[MC // 8 :]):
                value = jnp.zeros((8, 128), F32)
                for h in range(BLK_DEV // 128):
                    table = p_ref[j : j + 8, h * 128 : (h + 1) * 128]
                    got = jnp.take_along_axis(table, lo7, axis=1, mode="promise_in_bounds")
                    value = jnp.where(hi7 == h, got, value)
                total = total + value * kj
            vals_ref[pl.ds(2 * s, 1), :] = jnp.sum(total, axis=0, keepdims=True)

    def fetch_two(t, carry):
        fetch(g1_ref, 2 * t + 1)
        use(g0_ref, 2 * t)
        fetch(g0_ref, 2 * t + 2)
        use(g1_ref, 2 * t + 1)
        return carry

    last = SRC // CF - 1
    fetch(g0_ref, 0)
    lax.fori_loop(0, last // 2, fetch_two, 0)
    fetch(g1_ref, last)
    use(g0_ref, last - 1)
    use(g1_ref, last)


def owner_call(first, *args):
    outs = [
        jax.ShapeDtypeStruct((CC, BLK_DEV), F32),
        jax.ShapeDtypeStruct((2 * SRC, 128), F32),
        jax.ShapeDtypeStruct((1, 128), F32),
    ]
    if first:
        outs.append(jax.ShapeDtypeStruct((SRC, 128), jnp.int32))
    return pl.pallas_call(
        functools.partial(owner_kernel, first),
        out_shape=tuple(outs),
        scratch_shapes=[
            pltpu.VMEM((LO, SRC * 128), BF16),
            pltpu.VMEM((2 * HI * CC, CA * 128), BF16),
            pltpu.VMEM((2 * HI * CC, CA * 128), BF16),
            pltpu.VMEM((2 * HI * CC, LO), F32),
            pltpu.VMEM((2 * HI * MC, LO), BF16),
            pltpu.VMEM((2 * HI * MC, CF * 128), F32),
            pltpu.VMEM((2 * HI * MC, CF * 128), F32),
        ],
        compiler_params=pltpu.CompilerParams(vmem_limit_bytes=32 << 20),
        name="owner",
    )(*args)


def window_kernel(vals_ref, ray_ref, q_ref, beta_ref, wts_ref, qout_ref, alpha_ref, norm_ref, a_ref, b_ref):
    alpha = jnp.sqrt(jnp.sum(rows(vals_ref, 1, SRC, 2), axis=0, keepdims=True))
    alpha_ref[...] = alpha
    vals = rows(vals_ref, 0, N_WIN, 4) + rows(vals_ref, 2, N_WIN, 4)
    v1 = vals.astype(BF16).astype(F32)
    v2 = (vals - v1).astype(BF16).astype(F32)
    v3 = vals - v1 - v2
    ray = ray_ref[...]
    lo = jnp.bitwise_and(ray, 127).astype(F32)
    hi = jnp.right_shift(ray, 7)
    sub = lax.broadcasted_iota(jnp.int32, (8, 128), 0)
    tier = jnp.bitwise_and(sub, RT - 1)
    lo_iota = lax.broadcasted_iota(jnp.int32, (128, 128), 0).astype(F32).astype(BF16)
    ones, zeros = jnp.ones((128, 128), BF16), jnp.zeros((128, 128), BF16)
    wide = lambda r, p, n: jnp.broadcast_to(r[p : p + 1], (n, 128))
    for p in range(N_WIN):
        at = slice(p * 128, (p + 1) * 128)
        hit = tier == wide(hi, p, 8)
        upper = jnp.where(sub < RT, wide(v1, p, 8), wide(v2, p, 8))
        lower = jnp.where(sub < RT, wide(v3, p, 8), 0.0)
        both = jnp.concatenate([jnp.where(hit, upper, 0.0), jnp.where(hit, lower, 0.0)], axis=0)
        a_ref[:, at] = both.astype(BF16)
        b_ref[:, at] = jnp.where(lo_iota == wide(lo, p, 128).astype(BF16), ones, zeros)
    out = lax.dot_general(a_ref[...], b_ref[...], (((1,), (1,)), ((), ())), preferred_element_type=F32)
    summed = out[0:RT] + out[RT : 2 * RT] + out[2 * RT : 3 * RT]
    alpha_b = jnp.broadcast_to(alpha, (RT, 128))
    beta_b = jnp.broadcast_to(beta_ref[...], (RT, 128))
    q = summed / alpha_b - alpha_b * (q_ref[...] / beta_b)
    qout_ref[...] = q
    part = jnp.sum(q * q)
    weights = ray_values(q, ray)
    wts_ref[pl.ds(0, N_WIN, stride=4), :] = weights
    wts_ref[pl.ds(2, N_WIN, stride=4), :] = weights
    wts_ref[pl.ds(1, SRC, stride=2), :] = jnp.full((SRC, 128), part, F32)
    norm_ref[...] = jnp.full((SRC, 128), part, F32)


def window_call(vals, ray, q, beta):
    return pl.pallas_call(
        window_kernel,
        out_shape=(
            jax.ShapeDtypeStruct((2 * SRC, 128), F32),
            jax.ShapeDtypeStruct((RT, 128), F32),
            jax.ShapeDtypeStruct((1, 128), F32),
            jax.ShapeDtypeStruct((SRC, 128), F32),
        ),
        scratch_shapes=[
            pltpu.VMEM((16, N_WIN * 128), BF16),
            pltpu.VMEM((128, N_WIN * 128), BF16),
        ],
        compiler_params=pltpu.CompilerParams(vmem_limit_bytes=8 << 20),
        name="window",
    )(vals, ray, q, beta)


def end_kernel(norm_ref, q_ref, *refs):
    mine, theirs = refs[0:ITERS], refs[ITERS : 2 * ITERS]
    alphas = [r[...] for r in refs[2 * ITERS : 3 * ITERS]]
    betas = [r[...] for r in refs[3 * ITERS : 4 * ITERS]]
    update_ref, data_ref = refs[4 * ITERS :]
    betas.append(jnp.sqrt(jnp.sum(norm_ref[...], axis=0, keepdims=True)))
    data_ref[...] = q_ref[...] / jnp.broadcast_to(betas[ITERS], (RT, 128))
    one = jnp.ones_like(alphas[0])
    phibar, rhobar = betas[0], alphas[0]
    search = [one]
    update = [jnp.zeros_like(one) for _ in range(ITERS)]
    for step in range(ITERS):
        beta = betas[step + 1]
        rho = jnp.sqrt(rhobar * rhobar + beta * beta)
        cosine = rhobar / rho
        sine = beta / rho
        phi = cosine * phibar
        phibar = sine * phibar
        for i, s in enumerate(search):
            update[i] = update[i] + phi / rho * s
        if step + 1 < ITERS:
            theta = sine * alphas[step + 1]
            rhobar = -cosine * alphas[step + 1]
            search = [-(theta / rho * s) for s in search] + [one]
    scale = [jnp.broadcast_to(u / a, (CC, 128)) for u, a in zip(update, alphas)]
    core = lax.axis_index("off")
    for refs_in, half in ((mine, core), (theirs, 1 - core)):
        at = pl.ds(pl.multiple_of(half * CC, CC), CC)
        for t in range(BLK_DEV // 128):
            cols = slice(t * 128, (t + 1) * 128)
            total = refs_in[0][:, cols] * scale[0]
            for i in range(1, ITERS):
                total = total + refs_in[i][:, cols] * scale[i]
            update_ref[at, cols] = total


def end_call(norm, q, mine, theirs, alphas, betas):
    return pl.pallas_call(
        end_kernel,
        out_shape=(
            jax.ShapeDtypeStruct((CELLS, BLK_DEV), F32),
            jax.ShapeDtypeStruct((RT, 128), F32),
        ),
        compiler_params=pltpu.CompilerParams(vmem_limit_bytes=8 << 20),
        name="end",
    )(norm, q, *mine, *theirs, *alphas, *betas)


def exchange(x):
    rest = x.shape[0] // SRC
    y = lax.all_to_all(x.reshape(SRC, rest, 128), ("win", "off"), 0, 0, tiled=True)
    return y.reshape(x.shape)


def body(kernels, blocks, counts, ray_of, slopes):
    ray = ray_of.reshape(N_WIN, CAP)
    q = slopes.reshape(RT, 128)
    k = start_call(
        kernels.reshape(SRC, CC // 4, 4, CAP), blocks.reshape(N_WIN, CAP), counts.reshape(1, N_WIN), ray, q
    )
    k = lax.all_to_all(k, ("win", "off"), 0, 0, tiled=True).reshape(SRC * SLAB, CAP)
    mine, theirs, alphas, betas = [], [], [], []
    for step in range(ITERS):
        if step == 0:
            prev, vals, beta, ids = owner_call(True, k)
        else:
            prev, vals, beta = owner_call(False, k, ids, weights, prev, alpha)
        mine.append(prev)
        theirs.append(lax.ppermute(prev, "off", [(0, 1), (1, 0)]))
        betas.append(beta)
        weights, q, alpha, norm = window_call(exchange(vals), ray, q, beta)
        alphas.append(alpha)
        weights = exchange(weights)
    owner_call(False, k, ids, weights, prev, alpha)
    update, data = end_call(exchange(norm), q, mine, theirs, alphas, betas)
    return update, data.reshape(1, 1, RAYS)


def solution(mesh):
    in_specs = (
        P("off", "win", None, None, None),
        P("off", "win", None, None),
        P("off", "win", None),
        P("off", "win", None, None),
        P("off", "win", None),
    )
    out_specs = (P(None, "win"), P("off", "win", None))
    return jax.shard_map(body, mesh=mesh, in_specs=in_specs, out_specs=out_specs, check_vma=False)
```
